32 devices in a mesh: pipe: 4 (over x, core), seq: 8 (over z, y).
Axes of the slice: x: 2, y: 2, z: 4, core: 2. Of those that a mesh axis runs over, the one named last changes fastest.
Arguments:
- value_in: bfloat16 [4, 1024, 4096], P('pipe', 'seq'), may hold values from -6 to 6
- gate_one: bfloat16 [4, 1024, 4096], P('pipe', 'seq'), may hold values from -6 to 6
- gate_two: bfloat16 [4, 1024, 4096], P('pipe', 'seq'), may hold values from -6 to 6
- out_grad: bfloat16 [4, 1024, 4096], P('pipe', 'seq'), may hold values from -6 to 6
- w_embed: float32 [4, 33, 64], P('pipe'), may hold values from -1 to 1
- b_embed: float32 [4, 64], P('pipe'), may hold values from -4 to 4
- w_filter: float32 [4, 64, 4096], P('pipe', None, 'seq'), may hold values from -0.75 to 0.75
- decay: float32 [4, 4096], P('pipe', 'seq'), may hold values from 0.3 to 128
- skip: float32 [4, 4096], P('pipe', 'seq'), may hold values from -4 to 4
Outputs:
- next_input: bfloat16 [4, 1024, 4096], P('pipe', 'seq')
- grad_value: bfloat16 [4, 1024, 4096], P('pipe', 'seq')
- grad_gate_one: bfloat16 [4, 1024, 4096], P('pipe', 'seq')
- grad_gate_two: bfloat16 [4, 1024, 4096], P('pipe', 'seq')
- grad_w_embed: float32 [4, 33, 64], P('pipe')
- grad_b_embed: float32 [4, 64], P('pipe')
- grad_w_filter: float32 [4, 64, 4096], P('pipe', None, 'seq')
- grad_decay: float32 [4, 4096], P('pipe', 'seq')
- grad_skip: float32 [4, 4096], P('pipe', 'seq')
The draws below stay inside these ranges and needn't reach their ends.
All inputs are finite; a program needn't handle non-finite values.
Results may differ from the reference program's by a relative error of at most 0.0058.
Values may be sent and summed in bfloat16 or wider, within the bound.
A program may use at most 128 MiB of HBM per device.

```python
import math
import jax
import jax.numpy as jnp
from jax import lax

C = 4096
F = 64
E = 33
TOKENS = 1024
SECTIONS = 4


def levels(key, extent, split, low, largest):
    factor_of = 1.0
    for position, shards_of in split:
        draws = jax.random.uniform(jax.random.fold_in(jax.random.fold_in(key, 6), position), (shards_of,), jnp.float32, low / len(split), largest / len(split))
        factor_of = factor_of * jnp.repeat(jnp.exp(draws), extent[position] // shards_of).reshape((-1,) + (1,) * (len(extent) - 1 - position))
    return factor_of


def scatter_about(rng, dims, spread, reach, pieces=(), held_as=jnp.bfloat16):
    values = jax.random.normal(rng, dims, jnp.float32) * spread
    if len(pieces) > 0:
        values = levels(rng, dims, pieces, -0.22, 0.18) * values
    return jnp.clip(values, min=-reach, max=reach).astype(held_as)


def setup_inputs(seed: int = 0) -> dict:
    splits = jax.random.split(jax.random.key(seed), 10)
    value_in = scatter_about(splits[0], (SECTIONS, TOKENS, C), 1.0, 6.0, ((0, 4), (1, 8)))
    gate_one = scatter_about(splits[1], (SECTIONS, TOKENS, C), 1.0, 6.0, ((0, 4), (1, 8)))
    gate_two = scatter_about(splits[2], (SECTIONS, TOKENS, C), 1.0, 6.0, ((0, 4), (1, 8)))
    out_grad = scatter_about(splits[3], (SECTIONS, TOKENS, C), 1.0, 6.0, ((0, 4), (1, 8)))
    w_embed = scatter_about(splits[4], (SECTIONS, E, F), E ** -0.5, 1.0, ((0, 4),), jnp.float32)
    b_embed = scatter_about(splits[5], (SECTIONS, F), 1.0, 4.0, ((0, 4),), jnp.float32)
    w_filter = scatter_about(splits[6], (SECTIONS, F, C), F ** -0.5, 0.75, ((0, 4), (2, 8)), jnp.float32)
    decay = jnp.clip(jnp.exp(math.log(128.0) - 6.056003 * jax.random.uniform(splits[7], (SECTIONS, C), jnp.float32) ** levels(splits[7], (SECTIONS, C), ((0, 4), (1, 8)), -0.2, 0.2)), 0.3, 128.0)
    skip = scatter_about(splits[8], (SECTIONS, C), 1.0, 4.0, ((0, 4), (1, 8)), jnp.float32)
    return {"value_in": value_in, "gate_one": gate_one, "gate_two": gate_two, "out_grad": out_grad, "w_embed": w_embed, "b_embed": b_embed, "w_filter": w_filter, "decay": decay, "skip": skip}


def contract(form, left, right):
    return jnp.einsum(form, left, right, precision=lax.Precision.HIGHEST)

def position_features(length):
    position_ids = jnp.arange(length, dtype=jnp.int32)
    band_count = (E - 1) // 2
    band_index = jnp.arange(1, band_count + 1, dtype=jnp.int32)
    turn_ids = band_index[:, None] * band_index[:, None] * position_ids[None, :] % length
    angles = 2.0 * math.pi / length * turn_ids.astype(jnp.float32)
    position_ramp = position_ids.astype(jnp.float32)[None, :] / length
    return jnp.concatenate([position_ramp, jnp.cos(angles), jnp.sin(angles)], axis=0)

def section(inputs):
    values, gate_first, gate_second, cotangent, embed_w, embed_b, filter_w, decay_rate, skip_w = inputs
    length = values.shape[0]
    width = values.shape[1]
    blocks = 8
    block_width = width // blocks
    fft_total = 2 * length
    features = position_features(length)
    preact = contract('ef,et->ft', embed_w, features) + embed_b[:, None]
    activation = jnp.sin(preact)
    weighted = (values.astype(jnp.float32) * gate_first.astype(jnp.float32)).astype(jnp.bfloat16)
    upstream = (cotangent.astype(jnp.float32) * gate_second.astype(jnp.float32)).astype(jnp.bfloat16)
    positions = jnp.arange(length, dtype=jnp.int32).astype(jnp.float32)[:, None]

    def split_blocks(field):
        return jnp.moveaxis(field.reshape(field.shape[0], blocks, block_width), 1, 0)

    def merge_blocks(field):
        return jnp.moveaxis(field, 0, 1).reshape(field.shape[1], width)

    def one_block(parts):
        weighted_b, upstream_b, filter_b, decay_b, skip_b = parts
        weighted_f = weighted_b.astype(jnp.float32)
        upstream_f = upstream_b.astype(jnp.float32)
        envelope = jnp.exp(-decay_b[None, :] * positions / length) * (1.0 / math.sqrt(length))
        kernel = contract('ft,fc->tc', activation, filter_b) * envelope
        kernel_spec = jnp.fft.rfft(kernel, n=fft_total, axis=0)
        weighted_spec = jnp.fft.rfft(weighted_f, n=fft_total, axis=0)
        upstream_spec = jnp.fft.rfft(upstream_f, n=fft_total, axis=0)
        conv = jnp.fft.irfft(kernel_spec * weighted_spec, n=fft_total, axis=0)[:length]
        mixed_b = (conv + skip_b[None, :] * weighted_f).astype(jnp.bfloat16)
        backward_conv = jnp.fft.irfft(jnp.conj(kernel_spec) * upstream_spec, n=fft_total, axis=0)[:length]
        grad_weighted_b = (backward_conv + skip_b[None, :] * upstream_f).astype(jnp.bfloat16)
        grad_skip_b = lax.optimization_barrier(jnp.sum(upstream_f * weighted_f, axis=0))
        grad_kernel = jnp.fft.irfft(jnp.conj(weighted_spec) * upstream_spec, n=fft_total, axis=0)[:length]
        grad_decay_b = lax.optimization_barrier(jnp.sum(grad_kernel * kernel * (-positions / length), axis=0))
        grad_raw = grad_kernel * envelope
        grad_filter_b = contract('ft,tc->fc', activation, grad_raw)
        grad_act_b = contract('fc,tc->ft', filter_b, grad_raw)
        return (mixed_b, grad_weighted_b, grad_skip_b, grad_decay_b, grad_filter_b, grad_act_b)
    filter_blocks = jnp.moveaxis(filter_w.reshape(F, blocks, block_width), 1, 0)
    mixed_all, grad_weighted_all, skip_all, decay_all, filter_all, act_all = lax.map(one_block, (split_blocks(weighted), split_blocks(upstream), filter_blocks, decay_rate.reshape(blocks, block_width), skip_w.reshape(blocks, block_width)))
    mixed = merge_blocks(mixed_all)
    grad_weighted = merge_blocks(grad_weighted_all)
    grad_preact = lax.optimization_barrier(jnp.sum(act_all, axis=0)) * jnp.cos(preact)
    grad_embed_w = contract('et,ft->ef', features, grad_preact)
    grad_embed_b = lax.optimization_barrier(jnp.sum(grad_preact, axis=1))
    grad_filter_w = jnp.moveaxis(filter_all, 0, 1).reshape(F, width)
    output = (gate_second.astype(jnp.float32) * mixed.astype(jnp.float32)).astype(jnp.bfloat16)
    grad_values = (grad_weighted.astype(jnp.float32) * gate_first.astype(jnp.float32)).astype(jnp.bfloat16)
    grad_first = (grad_weighted.astype(jnp.float32) * values.astype(jnp.float32)).astype(jnp.bfloat16)
    grad_second = (cotangent.astype(jnp.float32) * mixed.astype(jnp.float32)).astype(jnp.bfloat16)
    return (output, grad_values, grad_first, grad_second, grad_embed_w, grad_embed_b, grad_filter_w, decay_all.reshape(width), skip_all.reshape(width))

def reference(value_in, gate_one, gate_two, out_grad, w_embed, b_embed, w_filter, decay, skip):
    results = lax.map(section, (value_in, gate_one, gate_two, out_grad, w_embed, b_embed, w_filter, decay, skip))
    output, grad_values, grad_first, grad_second, grad_embed_w, grad_embed_b, grad_filter_w, grad_decay, grad_skip = results
    next_input = jnp.roll(output, 1, axis=0)
    grad_value = jnp.roll(grad_values, -1, axis=0)
    grad_gate_one = jnp.roll(grad_first, -1, axis=0)
    grad_gate_two = jnp.roll(grad_second, -1, axis=0)
    return (next_input, grad_value, grad_gate_one, grad_gate_two, grad_embed_w, grad_embed_b, grad_filter_w, grad_decay, grad_skip)
```

```python
import functools
import math

import jax
import jax.numpy as jnp
import numpy as np
from jax import lax
from jax.experimental import pallas as pl
from jax.experimental.pallas import tpu as pltpu
from jax.sharding import PartitionSpec as P

E = 33


def from_behind(value, axis, steps):
    count = lax.axis_size(axis)
    pairs = [(source, (source + steps) % count) for source in range(count)]
    return lax.ppermute(value, axis, pairs)


def contract(form, left, right):
    return jnp.einsum(form, left, right, precision=lax.Precision.HIGHEST)


def position_features(length):
    position_ids = jnp.arange(length, dtype=jnp.int32)
    band_count = (E - 1) // 2
    band_index = jnp.arange(1, band_count + 1, dtype=jnp.int32)
    turn_ids = band_index[:, None] * band_index[:, None] * position_ids[None, :] % length
    angles = 2.0 * math.pi / length * turn_ids.astype(jnp.float32)
    position_ramp = position_ids.astype(jnp.float32)[None, :] / length
    return jnp.concatenate([position_ramp, jnp.cos(angles), jnp.sin(angles)], axis=0)


def build_tables(length):
    fft_total = 2 * length
    outer_len = 128
    half_len = outer_len // 2
    kept_len = half_len + 1
    inner_len = fft_total // outer_len
    index_kept = jnp.arange(kept_len, dtype=jnp.int32)
    index_half = jnp.arange(half_len, dtype=jnp.int32)
    index_inner = jnp.arange(inner_len, dtype=jnp.int32)
    angle_outer = (
        2.0
        * math.pi
        / outer_len
        * (index_kept[:, None] * index_half[None, :] % outer_len).astype(jnp.float32)
    )
    cos_outer = jnp.cos(angle_outer)
    sin_outer = jnp.sin(angle_outer)
    table_first = jnp.concatenate([cos_outer, -sin_outer], axis=0)
    angle_twist = (
        2.0
        * math.pi
        / fft_total
        * (index_kept[:, None] * index_inner[None, :] % fft_total).astype(jnp.float32)
    )
    cos_twist = jnp.cos(angle_twist)[:, :, None]
    sin_twist = jnp.sin(angle_twist)[:, :, None]
    angle_inner = (
        2.0
        * math.pi
        / inner_len
        * (index_inner[:, None] * index_inner[None, :] % inner_len).astype(jnp.float32)
    )
    cos_inner = jnp.cos(angle_inner)
    sin_inner = jnp.sin(angle_inner)
    table_second = jnp.stack(
        [jnp.stack([cos_inner, sin_inner], axis=1), jnp.stack([-sin_inner, cos_inner], axis=1)],
        axis=0,
    )
    table_back = jnp.stack(
        [jnp.stack([cos_inner, -sin_inner], axis=1), jnp.stack([sin_inner, cos_inner], axis=1)],
        axis=0,
    )
    weight_kept = (
        jnp.where((index_kept == 0) | (index_kept == half_len), 1.0, 2.0).astype(jnp.float32)
        / fft_total
    )
    table_last = jnp.stack(
        [
            jnp.transpose(cos_outer) * weight_kept[None, :],
            -jnp.transpose(sin_outer) * weight_kept[None, :],
        ],
        axis=1,
    )
    return (
        table_first,
        cos_twist,
        sin_twist,
        table_second,
        table_back,
        table_last,
        half_len,
        kept_len,
        inner_len,
    )


def staged_forward(field, tables_all):
    (
        table_first,
        cos_twist,
        sin_twist,
        table_second,
        table_back,
        table_last,
        half_len,
        kept_len,
        inner_len,
    ) = tables_all
    columns = field.shape[1]
    shaped = field.reshape(half_len, inner_len, columns)
    stacked = contract("kn,npc->kpc", table_first, shaped)
    part_re = stacked[:kept_len]
    part_im = stacked[kept_len:]
    twisted = jnp.stack(
        [part_re * cos_twist + part_im * sin_twist, part_im * cos_twist - part_re * sin_twist],
        axis=0,
    )
    return contract("sqrp,rkpc->skqc", table_second, twisted)


def staged_inverse(spec, tables_all):
    (
        table_first,
        cos_twist,
        sin_twist,
        table_second,
        table_back,
        table_last,
        half_len,
        kept_len,
        inner_len,
    ) = tables_all
    columns = spec.shape[3]
    sectioned = contract("sprq,rkqc->skpc", table_back, spec)
    section_re = sectioned[0]
    section_im = sectioned[1]
    twisted = jnp.stack(
        [
            section_re * cos_twist - section_im * sin_twist,
            section_im * cos_twist + section_re * sin_twist,
        ],
        axis=0,
    )
    result = contract("nrk,rkpc->npc", table_last, twisted)
    return result.reshape(half_len * inner_len, columns)


ROWS = 128
LEVEL = 2 * ROWS
PADDED = 40
LEVELS = 4
CW = 256
AHEAD = 3
TILE = 16


def level_tables():
    odd = 2 * np.arange(LEVEL) + 1
    shift = np.arange(-LEVEL, LEVEL)
    unit = math.pi / (2 * LEVEL)
    angle = unit * ((odd[:, None] * shift[None]) % (4 * LEVEL))
    ahead = np.concatenate([np.cos(angle), -np.sin(angle)], axis=0)
    back = ahead.T / LEVEL
    back = np.concatenate([back[LEVEL:], back[:LEVEL]], axis=1)
    return jnp.asarray(ahead, jnp.bfloat16), jnp.asarray(back, jnp.bfloat16)


def padded_features(length):
    position = np.arange(length)
    band = np.arange(1, (E - 1) // 2 + 1)
    angle = 2.0 * math.pi / length * ((band[:, None] ** 2 * position[None]) % length)
    table = np.zeros((PADDED, length), np.float32)
    table[0] = position / length
    table[1 : 1 + len(band)] = np.cos(angle)
    table[1 + len(band) : E] = np.sin(angle)
    table[E] = 1.0
    return table


def section_kernel(
    pipes, per,
    v_in, g1_in, og_in, g2_in, feat_in, feat_t_in, ahead_in, back_in,
    wf, decay, skip, w_embed, bias,
    o_next, o_val, o_first, o_second, o_emb, o_wf, o_decay, o_skip,
    ins, taken, feat, feat_t, ahead, back, ahead_k, back_g, wext, act, act_t, cos_t,
    wf_all, row_all, lev, ysend, near1, far1, far2, cin, cout, olev, mland, gland,
    mstage, gstage, fpart, kb, env, kap, spec, prod, corr, graw, gact,
    wf_send, row_send, wf_recv, row_recv, wf_own, row_own, part, parts,
    loaded, y_s, y_r, z_s, z_r, c_s, c_r, m_s, m_r, g_s, g_r, p_s, p_r, o_s,
    wf_s, wf_r, row_s, row_r, gw_s, gw_r, sum_s, sum_r, t_s, t_r, x_s, x_r,
):
    f32, bf16 = jnp.float32, jnp.bfloat16
    length = LEVELS * LEVEL
    width = wf.shape[1]
    hidden = wf.shape[0]
    shards = 2 * LEVELS
    steps = LEVELS * per
    pipe = lax.axis_index("pipe")
    me = lax.axis_index("seq")
    z, y = me // 2, me % 2
    twin = 1 - y
    partner = 2 * z + twin
    near = z // 2
    far = 1 - near
    adjacent = z + 1 - 2 * (z % 2)
    inner = (z == 1) | (z == 2)
    outer = (z == 0) | (z == 3)
    nxt = (pipe + 1) % pipes
    prv = (pipe + pipes - 1) % pipes
    high = lax.Precision.HIGHEST
    sign = (1 - 2 * near).astype(f32)

    def rows(index):
        return pl.ds(pl.multiple_of(index * ROWS, ROWS), ROWS)

    def cols(step, lane):
        block = (2 * (step // per) + lane) * per + step % per
        return pl.ds(pl.multiple_of(block * CW, CW), CW)

    def sub(step):
        return pl.ds(pl.multiple_of((step % per) * CW, CW), CW)

    def remote(src, dst, send, recv, there):
        return pltpu.make_async_remote_copy(
            src_ref=src, dst_ref=dst, send_sem=send, recv_sem=recv, device_id=there,
            device_id_type=pl.DeviceIdType.MESH,
        )

    def at_level(level):
        return (pipe, 2 * level + y)

    def crossing(kind, step):
        return remote(
            ysend.at[kind, step], lev.at[kind, step, rows(y), :],
            y_s.at[kind, step], y_r.at[kind, step], (pipe, partner),
        )

    def crossed(kind, step):
        return remote(
            ysend.at[kind, step], lev.at[kind, step, rows(twin), :],
            y_s.at[kind, step], y_r.at[kind, step], (pipe, partner),
        )

    def upward(slot, step, buffer, level, send):
        return remote(
            lev.at[near, step], buffer.at[step], z_s.at[send, step], z_r.at[slot, step],
            at_level(level),
        )

    def given(step):
        return remote(
            cout.at[step], cin.at[step], c_s.at[step], c_r.at[step], at_level(adjacent)
        )

    def homeward(step):
        return remote(
            olev.at[0, step, rows(twin), :], mland.at[step], m_s.at[step], m_r.at[step],
            (pipe, partner),
        )

    def backward(side, step):
        return remote(
            olev.at[1, step, rows(side), :], gland.at[y, step], g_s.at[side, step],
            g_r.at[y, step], (prv, 2 * z + side),
        )

    def arrived_grad(lane, step):
        return remote(
            olev.at[1, step, rows(lane), :], gland.at[lane, step], g_s.at[lane, step],
            g_r.at[lane, step], (prv, 2 * z + lane),
        )

    def handed(kind, side, step):
        out = (o_next, o_second)[kind]
        lane = (y, twin)[side]
        return remote(
            mstage.at[kind, side, step], out.at[:, cols(step, lane)],
            p_s.at[kind, side, step], p_r.at[kind, side, step],
            (nxt if kind == 0 else prv, me),
        )

    def written(kind, lane, step):
        out = (o_val, o_first)[kind]
        return pltpu.make_async_copy(
            gstage.at[kind, lane, step], out.at[:, cols(step, lane)], o_s.at[kind, lane, step]
        )

    def filters(there, source):
        return (
            remote(wf_all.at[source], wf_all.at[source], wf_s.at[there], wf_r.at[source],
                   at_level(there)),
            remote(row_all.at[source], row_all.at[source], row_s.at[there], row_r.at[source],
                   at_level(there)),
        )

    def partials(step, there, source):
        return (
            remote(wf_send.at[step], wf_recv.at[source, step % per], gw_s.at[step],
                   gw_r.at[source, step % per], at_level(there)),
            remote(row_send.at[step], row_recv.at[source, step % per], sum_s.at[step],
                   sum_r.at[source, step % per], at_level(there)),
        )

    def ahead_of_time(kind):
        return remote(ins.at[kind], taken.at[kind], t_s.at[kind], t_r.at[kind], (prv, me))

    def shared(there, source):
        return remote(part, parts.at[source], x_s.at[there], x_r.at[source], (pipe, there))

    def other_levels(visit):
        def body(step, carry):
            visit((z + 1 + step) % LEVELS)
            return carry

        lax.fori_loop(0, LEVELS - 1, body, 0)

    def others(visit):
        def body(step, carry):
            visit((me + 1 + step) % shards)
            return carry

        lax.fori_loop(0, shards - 1, body, 0)

    def every(visit):
        def body(step, carry):
            visit(step)
            return carry

        lax.fori_loop(0, steps, body, 0)

    loads = [
        pltpu.make_async_copy(src, dst, loaded.at[index])
        for index, (src, dst) in enumerate((
            (v_in, ins.at[0]), (g1_in, ins.at[1]), (og_in, ins.at[2]), (g2_in, ins.at[3]),
            (feat_in, feat), (feat_t_in, feat_t), (ahead_in, ahead), (back_in, back),
        ))
    ]
    for load in loads:
        load.start()
    barrier = pltpu.get_barrier_semaphore()

    def greet(there):
        pl.semaphore_signal(
            barrier, inc=1, device_id=(pipe, there), device_id_type=pl.DeviceIdType.MESH
        )

    others(greet)
    for beside in (nxt, prv):
        for there in (me, partner):
            pl.semaphore_signal(
                barrier, inc=1, device_id=(beside, there), device_id_type=pl.DeviceIdType.MESH
            )
    wf_all[z] = wf[...].astype(bf16)
    row_all[z, 0:1, :] = decay[...]
    row_all[z, 1:2, :] = skip[...]
    wext[...] = jnp.zeros_like(wext)
    wext[:E, :hidden] = w_embed[:, 0, :]
    wext[:E, hidden:] = w_embed[:, 0, :]
    wext[E : E + 1, :hidden] = bias[...]
    wext[E : E + 1, hidden:] = bias[...]
    kb[:LEVEL, :] = jnp.zeros((LEVEL, CW), bf16)
    gact[...] = jnp.zeros_like(gact)
    for load in loads[:4]:
        load.wait()

    def times(kind, here):
        left, right = ins[2 * kind, :, here], ins[2 * kind + 1, :, here]
        return (left.astype(f32) * right.astype(f32)).astype(bf16)

    def weigh(step):
        for kind in (0, 1):
            ysend[kind, step] = times(kind, cols(step, twin))
            lev[kind, step, rows(y), :] = times(kind, cols(step, y))

    every(weigh)
    pl.semaphore_wait(barrier, shards + 3)

    def send_filters(there):
        for copy in filters(there, z):
            copy.start()

    other_levels(send_filters)

    def cross(step):
        crossing(near, step).start()
        crossing(far, step).start()

    every(cross)
    for kind in range(2):
        ahead_of_time(kind).start()

    def climb(step):
        crossed(near, step).wait_recv()

        @pl.when(inner)
        def _():
            upward(1, step, far1, 3 - z, 0).start()

        @pl.when(outer)
        def _():
            upward(0, step, near1, adjacent, 0).start()
            upward(2, step, far2, 3 - adjacent, 1).start()

    climb(0)
    for load in loads[4:]:
        load.wait()
    ahead_k[:LEVEL, :] = ahead[:LEVEL, :]
    ahead_k[LEVEL:, :] = (ahead[LEVEL:, :].astype(f32) * sign).astype(bf16)
    for block in range(4):
        here = slice(block * LEVEL, (block + 1) * LEVEL)
        flip = sign if block % 2 else 1.0
        back_g[:, here] = (back[:, here].astype(f32) * flip).astype(bf16)

    def activate(block, carry):
        here = pl.ds(pl.multiple_of(block * LEVEL, LEVEL), LEVEL)
        lane = lax.broadcasted_iota(jnp.int32, (LEVEL, 2 * hidden), 1)
        value = jnp.sin(jnp.dot(feat_t[here, :], wext[...], precision=high))
        top = value.astype(bf16).astype(f32)
        act[here, :] = jnp.where(lane < hidden, top, value - top).astype(bf16)
        line = lax.broadcasted_iota(jnp.int32, (2 * hidden, LEVEL), 0)
        preact = lax.dot_general(
            wext[...], feat[:, here], (((0,), (0,)), ((), ())), precision=high
        )
        value = jnp.sin(preact)
        top = value.astype(bf16).astype(f32)
        act_t[:, here] = jnp.where(line < hidden, top, value - top).astype(bf16)
        cos_t[:, here] = jnp.cos(preact[:hidden])
        return carry

    lax.fori_loop(0, LEVELS, activate, 0)
    for step in range(1, AHEAD):
        climb(step)

    def land_filters(there):
        for copy in filters(there, there):
            copy.wait_recv()

    other_levels(land_filters)

    def filter_rows(step):
        return wf_all[step // per, :, sub(step)]

    def prepare(step, depth):
        weights = filter_rows(step)
        weights = jnp.concatenate([weights, weights], axis=0)
        rate = row_all[step // per, 0:1, sub(step)]
        fine = lax.broadcasted_iota(jnp.int32, (LEVEL, 1), 0).astype(f32)
        base = jnp.exp(-rate * fine / length) * (1.0 / math.sqrt(length))
        for block in range(depth):
            here = slice(block * LEVEL, (block + 1) * LEVEL)
            raw = jnp.dot(act[here, :], weights, preferred_element_type=f32)
            envelope = base * jnp.exp(rate * (-block * LEVEL / length)) if block else base
            env[here, :] = envelope
            kb[(block + 1) * LEVEL : (block + 2) * LEVEL, :] = (raw * envelope).astype(bf16)
        kap[0] = jnp.dot(
            ahead_k[:, LEVEL:], kb[LEVEL : 2 * LEVEL, :], preferred_element_type=f32
        )
        for block in range(1, depth):
            kap[block] = jnp.dot(
                ahead_k[...], kb[block * LEVEL : (block + 2) * LEVEL, :],
                preferred_element_type=f32,
            )

    def transform(slot, source):
        spec[slot] = jnp.dot(ahead[:, LEVEL:], source, preferred_element_type=f32)

    def inverse(slot):
        return jnp.dot(back[:, : 2 * LEVEL], prod[slot], preferred_element_type=f32)

    def forth(one, two):
        return one[0] * two[0] - one[1] * two[1], one[0] * two[1] + one[1] * two[0]

    def conj(one, two):
        return one[0] * two[0] + one[1] * two[1], one[0] * two[1] - one[1] * two[0]

    def add(*terms):
        total = terms[0]
        for term in terms[1:]:
            total = total[0] + term[0], total[1] + term[1]
        return total

    def half(one):
        return one[0] * 0.5, one[1] * 0.5

    def combine(visit):
        def body(tile, carry):
            top = pl.ds(pl.multiple_of(tile * TILE, TILE), TILE)
            low = pl.ds(pl.multiple_of(LEVEL + tile * TILE, TILE), TILE)

            def read(ref, index):
                return ref[index, top, :], ref[index, low, :]

            def write(ref, index, value):
                ref[index, top, :] = value[0].astype(bf16)
                ref[index, low, :] = value[1].astype(bf16)

            visit(read, write)
            return carry

        lax.fori_loop(0, LEVEL // TILE, body, 0)

    def combine_inner(read, write):
        k0, k1, k2, k3 = [read(kap, index) for index in range(4)]
        n0, n1, f0, f1, f2 = [read(spec, index) for index in range(5)]
        write(prod, 0, add(conj(k1, f0), conj(k2, f1), conj(k3, f2)))
        write(prod, 1, add(forth(k0, n0), forth(k1, n1)))
        write(prod, 2, add(conj(k0, f0), conj(k1, f1), conj(k2, f2)))
        write(corr, 0, conj(n0, f0))
        write(corr, 1, add(conj(n1, f0), conj(n0, half(f1))))
        write(corr, 2, conj(n0, f2))
        write(corr, 3, conj(half(n1), f2))

    def combine_outer(read, write):
        k0, n0, f0 = read(kap, 0), read(spec, 0), read(spec, 2)
        write(prod, 1, forth(k0, n0))
        write(prod, 2, conj(k0, f0))
        write(corr, 0, conj(n0, f0))

    def skipped(kind, step):
        return row_all[step // per, 1:2, sub(step)] * lev[kind, step].astype(f32)

    def pass_mixed(side, step):
        lane = (y, twin)[side]
        block = (olev[0, step, rows(y), :] if side == 0 else mland[step]).astype(f32)
        here = cols(step, lane)
        mstage[0, side, step] = (ins[3, :, here].astype(f32) * block).astype(bf16)
        mstage[1, side, step] = (ins[2, :, here].astype(f32) * block).astype(bf16)
        handed(0, side, step).start()
        handed(1, side, step).start()

    def send_mixed(step):
        homeward(step).start()
        pass_mixed(0, step)

    def send_grad(step):
        backward(0, step).start()
        backward(1, step).start()

    def land(step):
        homeward(step).wait_recv()
        pass_mixed(1, step)
        for lane in range(2):
            arrived_grad(lane, step).wait_recv()
            block = gland[lane, step].astype(f32)
            here = cols(step, lane)
            gstage[0, lane, step] = (taken[1, :, here].astype(f32) * block).astype(bf16)
            gstage[1, lane, step] = (taken[0, :, here].astype(f32) * block).astype(bf16)
            written(0, lane, step).start()
            written(1, lane, step).start()

    def correlate(step, depth):
        fine = lax.broadcasted_iota(jnp.int32, (LEVEL, 1), 0).astype(f32)
        total = jnp.zeros((1, CW), f32)
        for block in range(depth):
            here = slice(block * LEVEL, (block + 1) * LEVEL)
            grad = jnp.dot(back_g[:, : 2 * LEVEL], corr[block], preferred_element_type=f32)
            if block + 1 < depth:
                grad += jnp.dot(
                    back_g[:, 2 * LEVEL :], corr[block + 1], preferred_element_type=f32
                )
            graw[here, :] = (grad * env[here, :]).astype(bf16)
            kernel = kb[(block + 1) * LEVEL : (block + 2) * LEVEL, :].astype(f32)
            place = (fine + block * LEVEL) * (-1.0 / length)
            total += jnp.sum(grad * kernel * place, axis=0, keepdims=True)
        both = lev[0, step].astype(f32) * lev[1, step].astype(f32)
        skip_sum = jnp.sum(both, axis=0, keepdims=True)
        span = depth * LEVEL
        both = jnp.dot(act_t[:, :span], graw[:span, :], preferred_element_type=f32)
        share = both[:hidden] + both[hidden:]
        gact[:, :span] += lax.dot_general(
            filter_rows(step), graw[:span, :], (((1,), (1,)), ((), ())),
            preferred_element_type=f32,
        )
        owner = step // per

        @pl.when(owner == z)
        def _():
            wf_own[:, sub(step)] = share
            row_own[0:1, sub(step)] = total
            row_own[1:2, sub(step)] = skip_sum

        @pl.when(owner != z)
        def _():
            wf_send[step] = share.astype(bf16)
            row_send[step, 0:1, :] = total
            row_send[step, 1:2, :] = skip_sum
            for copy in partials(step, owner, z):
                copy.start()

    def climb_later(step):
        @pl.when(step + AHEAD < steps)
        def _():
            climb(step + AHEAD)

    for kind in range(2):
        ahead_of_time(kind).wait_recv()

    @pl.when(inner)
    def _():
        def turn(step):
            climb_later(step)
            prepare(step, LEVELS)
            transform(0, lev[near, step])
            crossed(far, step).wait_recv()
            transform(2, lev[far, step])
            upward(0, step, near1, adjacent, 0).wait_recv()
            transform(1, near1[step])
            upward(1, step, far1, 3 - z, 0).wait_recv()
            transform(3, far1[step])
            upward(2, step, far2, 3 - adjacent, 0).wait_recv()
            transform(4, far2[step])
            combine(combine_inner)
            cout[step] = inverse(0).astype(bf16)
            given(step).start()
            olev[near, step] = (inverse(1) + skipped(near, step)).astype(bf16)
            olev[far, step] = (inverse(2) + skipped(far, step)).astype(bf16)
            send_mixed(step)
            send_grad(step)
            correlate(step, LEVELS)

            @pl.when(step >= 1)
            def _():
                land(step - 1)

        every(turn)
        land(steps - 1)

    @pl.when(outer)
    def _():
        def settle(step):
            given(step).wait_recv()
            olev[far, step] = (fpart[step % 2] + cin[step].astype(f32)).astype(bf16)

            @pl.when(near == 0)
            def _():
                send_grad(step)

            @pl.when(near == 1)
            def _():
                send_mixed(step)

        def turn(step):
            climb_later(step)
            prepare(step, 1)
            transform(0, lev[near, step])
            crossed(far, step).wait_recv()
            transform(2, lev[far, step])
            combine(combine_outer)
            olev[near, step] = (inverse(1) + skipped(near, step)).astype(bf16)

            @pl.when(near == 0)
            def _():
                send_mixed(step)

            @pl.when(near == 1)
            def _():
                send_grad(step)

            fpart[step % 2] = inverse(2) + skipped(far, step)
            correlate(step, 1)

            @pl.when(step >= 1)
            def _():
                settle(step - 1)

            @pl.when(step >= 2)
            def _():
                land(step - 2)

        every(turn)
        settle(steps - 1)
        land(steps - 2)
        land(steps - 1)

    grad_pre = gact[...] * cos_t[...]
    part[...] = lax.dot_general(
        feat[...], jnp.concatenate([grad_pre, jnp.zeros_like(grad_pre)], axis=0),
        (((1,), (1,)), ((), ())), precision=high,
    )
    others(lambda there: shared(there, me).start())
    parts[me] = part[...]

    def gather(there):
        for piece in range(per):
            here = slice(piece * CW, (piece + 1) * CW)
            step = z * per + piece
            for copy in partials(step, there, there):
                copy.wait_recv()
            wf_own[:, here] += wf_recv[there, piece].astype(f32)
            row_own[0:2, here] += row_recv[there, piece, 0:2, :]

    other_levels(gather)
    o_wf[...] = wf_own[...]
    o_decay[...] = row_own[0:1, :]
    o_skip[...] = row_own[1:2, :]
    others(lambda source: shared(source, source).wait_recv())
    total = parts[0]
    for index in range(1, shards):
        total = total + parts[index]
    o_emb[...] = total

    def sent_filters(there):
        for copy in filters(there, z):
            copy.wait_send()

    other_levels(sent_filters)
    others(lambda there: shared(there, me).wait_send())
    for kind in range(2):
        ahead_of_time(kind).wait_send()

    def finish(step):
        for kind in (0, 1):
            crossing(kind, step).wait_send()
            backward(kind, step).wait_send()
            for side in (0, 1):
                handed(kind, side, step).wait()
                written(kind, side, step).wait()
        homeward(step).wait_send()

        @pl.when(step // per != z)
        def _():
            for copy in partials(step, step // per, z):
                copy.wait_send()

        @pl.when(inner)
        def _():
            given(step).wait_send()
            upward(1, step, far1, 3 - z, 0).wait_send()

        @pl.when(outer)
        def _():
            upward(0, step, near1, adjacent, 0).wait_send()
            upward(2, step, far2, 3 - adjacent, 1).wait_send()

    every(finish)


CHUNKS = 4


def finish_kernel(
    a_in, b_in, c_in, d_in, emb, wf, row_d, row_s,
    a_out, b_out, c_out, d_out, o_emb, o_bias, o_wf, o_d, o_s, held, got, put,
):
    rows = ROWS // CHUNKS
    reads, writes = [], []
    for kind, (src, dst) in enumerate(
        ((a_in, a_out), (b_in, b_out), (c_in, c_out), (d_in, d_out))
    ):
        for chunk in range(CHUNKS):
            here = pl.ds(chunk * rows, rows)
            index = kind * CHUNKS + chunk
            middle = held.at[kind, here, :]
            reads.append(pltpu.make_async_copy(src.at[here, :], middle, got.at[index]))
            writes.append(pltpu.make_async_copy(middle, dst.at[0, here, :], put.at[index]))
    for read in reads:
        read.start()
    o_emb[:, 0, :] = emb[:E, : o_emb.shape[2]]
    o_bias[...] = emb[E : E + 1, : o_bias.shape[1]]
    o_wf[0] = wf[...]
    o_d[...] = row_d[...]
    o_s[...] = row_s[...]
    for read, write in zip(reads, writes):
        read.wait()
        write.start()
    for write in writes:
        write.wait()


def fused_section(v, g1, g2, og, w_embed, b_embed, wf, decay, skip):
    pipes = lax.axis_size("pipe")
    shards = 2 * LEVELS
    length = LEVELS * LEVEL
    wide_cols = v.shape[1]
    hidden, width = wf.shape
    per = width // CW
    steps = LEVELS * per
    f32, bf16 = jnp.float32, jnp.bfloat16
    feat = padded_features(length)
    ahead, back = level_tables()
    vmem = pl.BlockSpec(memory_space=pltpu.VMEM)
    hbm = pl.BlockSpec(memory_space=pl.ANY)
    stream = jax.ShapeDtypeStruct((ROWS, wide_cols), bf16)
    row = jax.ShapeDtypeStruct((1, width), f32)
    dma = pltpu.SemaphoreType.DMA
    level = pltpu.VMEM((steps, LEVEL, CW), bf16)
    results = pl.pallas_call(
        functools.partial(section_kernel, pipes, per),
        out_shape=(
            stream, stream, stream, stream,
            jax.ShapeDtypeStruct((PADDED, 2 * hidden), f32),
            jax.ShapeDtypeStruct((hidden, width), f32), row, row,
        ),
        in_specs=[hbm] * 8 + [vmem] * 5,
        out_specs=(hbm,) * 4 + (vmem,) * 4,
        scratch_shapes=[
            pltpu.VMEM((4, ROWS, wide_cols), bf16),
            pltpu.VMEM((2, ROWS, wide_cols), bf16),
            pltpu.VMEM((PADDED, length), f32),
            pltpu.VMEM((length, PADDED), f32),
            pltpu.VMEM((2 * LEVEL, 2 * LEVEL), bf16),
            pltpu.VMEM((LEVEL, 4 * LEVEL), bf16),
            pltpu.VMEM((2 * LEVEL, 2 * LEVEL), bf16),
            pltpu.VMEM((LEVEL, 4 * LEVEL), bf16),
            pltpu.VMEM((PADDED, 2 * hidden), f32),
            pltpu.VMEM((length, 2 * hidden), bf16),
            pltpu.VMEM((2 * hidden, length), bf16),
            pltpu.VMEM((hidden, length), f32),
            pltpu.VMEM((LEVELS, hidden, width), bf16),
            pltpu.VMEM((LEVELS, 8, width), f32),
            pltpu.VMEM((2, steps, LEVEL, CW), bf16),
            pltpu.VMEM((2, steps, ROWS, CW), bf16),
            level, level, level, level, level,
            pltpu.VMEM((2, steps, LEVEL, CW), bf16),
            pltpu.VMEM((steps, ROWS, CW), bf16),
            pltpu.VMEM((2, steps, ROWS, CW), bf16),
            pltpu.VMEM((2, 2, steps, ROWS, CW), bf16),
            pltpu.VMEM((2, 2, steps, ROWS, CW), bf16),
            pltpu.VMEM((2, LEVEL, CW), f32),
            pltpu.VMEM((length + LEVEL, CW), bf16),
            pltpu.VMEM((length, CW), f32),
            pltpu.VMEM((LEVELS, 2 * LEVEL, CW), f32),
            pltpu.VMEM((5, 2 * LEVEL, CW), f32),
            pltpu.VMEM((3, 2 * LEVEL, CW), bf16),
            pltpu.VMEM((LEVELS, 2 * LEVEL, CW), bf16),
            pltpu.VMEM((length, CW), bf16),
            pltpu.VMEM((hidden, length), f32),
            pltpu.VMEM((steps, hidden, CW), bf16),
            pltpu.VMEM((steps, 8, CW), f32),
            pltpu.VMEM((LEVELS, per, hidden, CW), bf16),
            pltpu.VMEM((LEVELS, per, 8, CW), f32),
            pltpu.VMEM((hidden, width), f32),
            pltpu.VMEM((8, width), f32),
            pltpu.VMEM((PADDED, 2 * hidden), f32),
            pltpu.VMEM((shards, PADDED, 2 * hidden), f32),
            dma((8,)),
            dma((2, steps)), dma((2, steps)),
            dma((2, steps)), dma((3, steps)),
            dma((steps,)), dma((steps,)),
            dma((steps,)), dma((steps,)),
            dma((2, steps)), dma((2, steps)),
            dma((2, 2, steps)), dma((2, 2, steps)),
            dma((2, 2, steps)),
            dma((LEVELS,)), dma((LEVELS,)),
            dma((LEVELS,)), dma((LEVELS,)),
            dma((steps,)), dma((LEVELS, per)),
            dma((steps,)), dma((LEVELS, per)),
            dma((2,)), dma((2,)),
            dma((shards,)), dma((shards,)),
        ],
        compiler_params=pltpu.CompilerParams(
            collective_id=0, has_side_effects=True, vmem_limit_bytes=60 * 1024 * 1024
        ),
    )(
        v, g1, og, g2, jnp.asarray(feat), jnp.asarray(feat.T.copy()), ahead, back,
        wf, decay[None], skip[None], w_embed[:, None, :], b_embed[None],
    )
    final = jax.ShapeDtypeStruct((1, ROWS, wide_cols), bf16)
    done = pl.pallas_call(
        finish_kernel,
        out_shape=(
            final, final, final, final,
            jax.ShapeDtypeStruct((E, 1, hidden), f32),
            jax.ShapeDtypeStruct((1, hidden), f32),
            jax.ShapeDtypeStruct((1, hidden, width), f32), row, row,
        ),
        in_specs=[hbm] * 4 + [vmem] * 4,
        out_specs=(hbm,) * 4 + (vmem,) * 5,
        scratch_shapes=[
            pltpu.VMEM((4, ROWS, wide_cols), bf16),
            dma((4 * CHUNKS,)), dma((4 * CHUNKS,)),
        ],
        compiler_params=pltpu.CompilerParams(vmem_limit_bytes=60 * 1024 * 1024),
    )(*results)
    return done[:4] + (jnp.swapaxes(done[4], 0, 1),) + done[5:]


def spectral_product(left, right, conjugate_left):
    left_re = left[0]
    left_im = left[1]
    right_re = right[0]
    right_im = right[1]
    if conjugate_left:
        left_im = -left_im
    return jnp.stack(
        [left_re * right_re - left_im * right_im, left_re * right_im + left_im * right_re], axis=0
    )


def per_device(value_in, gate_one, gate_two, out_grad, w_embed, b_embed, w_filter, decay, skip):
    values = value_in[0]
    gate_first = gate_one[0]
    gate_second = gate_two[0]
    cotangent = out_grad[0]
    filter_w = w_filter[0]
    shards = lax.axis_size("seq")
    length = values.shape[0] * shards
    fits = length == 1024 and values.shape == (ROWS, 4096) and shards == 8
    if fits and lax.axis_size("pipe") > 2:
        return fused_section(
            values, gate_first, gate_second, cotangent,
            w_embed[0], b_embed[0], filter_w, decay[0], skip[0],
        )
    weighted = (values.astype(jnp.float32) * gate_first.astype(jnp.float32)).astype(jnp.bfloat16)
    upstream = (cotangent.astype(jnp.float32) * gate_second.astype(jnp.float32)).astype(
        jnp.bfloat16
    )
    features = position_features(length)
    preact = contract("ef,et->ft", w_embed[0], features) + b_embed[0][:, None]
    activation = jnp.sin(preact)
    positions = jnp.arange(length, dtype=jnp.int32).astype(jnp.float32)[:, None]
    envelope = jnp.exp(-decay[0][None, :] * positions / length) * (1.0 / math.sqrt(length))
    kernel = contract("ft,fc->tc", activation, filter_w) * envelope
    tables_all = build_tables(length)
    forward_transform, inverse_transform = staged_forward, staged_inverse
    kernel_spec = forward_transform(kernel, tables_all)
    skip_row = skip[0][None, :]
    weighted_chan, upstream_chan = (
        lax.all_to_all(weighted, "seq", split_axis=1, concat_axis=0, tiled=True),
        lax.all_to_all(upstream, "seq", split_axis=1, concat_axis=0, tiled=True),
    )
    weighted_f = weighted_chan.astype(jnp.float32)
    weighted_spec = forward_transform(weighted_f, tables_all)
    conv = inverse_transform(spectral_product(kernel_spec, weighted_spec, False), tables_all)
    mixed_chan, weighted_f, weighted_spec = (
        (conv + skip_row * weighted_f).astype(jnp.bfloat16),
        weighted_f,
        weighted_spec,
    )
    upstream_f = upstream_chan.astype(jnp.float32)
    upstream_spec = forward_transform(upstream_f, tables_all)
    backward_conv = inverse_transform(
        spectral_product(kernel_spec, upstream_spec, True), tables_all
    )
    grad_chan = (backward_conv + skip_row * upstream_f).astype(jnp.bfloat16)
    grad_skip = jnp.sum(upstream_f * weighted_f, axis=0)
    grad_kernel = inverse_transform(
        spectral_product(weighted_spec, upstream_spec, True), tables_all
    )
    grad_chan, grad_skip, grad_kernel = (grad_chan, grad_skip, grad_kernel)
    mixed_seq, grad_weighted = (
        lax.all_to_all(mixed_chan, "seq", split_axis=0, concat_axis=1, tiled=True),
        lax.all_to_all(grad_chan, "seq", split_axis=0, concat_axis=1, tiled=True),
    )
    output = (gate_second.astype(jnp.float32) * mixed_seq.astype(jnp.float32)).astype(jnp.bfloat16)
    next_input = from_behind(output, "pipe", 1)
    grad_decay = jnp.sum(grad_kernel * kernel * (-positions / length), axis=0)
    grad_raw = grad_kernel * envelope
    grad_filter_w = contract("ft,tc->fc", activation, grad_raw)
    grad_preact = contract("fc,tc->ft", filter_w, grad_raw) * jnp.cos(preact)
    part_weight = contract("et,ft->ef", features, grad_preact)
    part_bias = jnp.sum(grad_preact, axis=1)
    grad_embed_w, grad_embed_b = lax.psum((part_weight, part_bias), "seq")
    grad_values = (grad_weighted.astype(jnp.float32) * gate_first.astype(jnp.float32)).astype(
        jnp.bfloat16
    )
    grad_first = (grad_weighted.astype(jnp.float32) * values.astype(jnp.float32)).astype(
        jnp.bfloat16
    )
    grad_second = (cotangent.astype(jnp.float32) * mixed_seq.astype(jnp.float32)).astype(
        jnp.bfloat16
    )
    moved_values, moved_first, moved_second = from_behind(
        (grad_values, grad_first, grad_second), "pipe", -1
    )
    return (
        next_input[None],
        moved_values[None],
        moved_first[None],
        moved_second[None],
        grad_embed_w[None],
        grad_embed_b[None],
        grad_filter_w[None],
        grad_decay[None],
        grad_skip[None],
    )


def solution(mesh):
    return jax.shard_map(
        per_device,
        mesh=mesh,
        in_specs=(
            P("pipe", "seq", None),
            P("pipe", "seq", None),
            P("pipe", "seq", None),
            P("pipe", "seq", None),
            P("pipe", None, None),
            P("pipe", None),
            P("pipe", None, "seq"),
            P("pipe", "seq"),
            P("pipe", "seq"),
        ),
        out_specs=(
            P("pipe", "seq", None),
            P("pipe", "seq", None),
            P("pipe", "seq", None),
            P("pipe", "seq", None),
            P("pipe", None, None),
            P("pipe", None),
            P("pipe", None, "seq"),
            P("pipe", "seq"),
            P("pipe", "seq"),
        ),
        check_vma=False,
    )
```

```python
import functools
import math

import jax
import jax.numpy as jnp
import numpy as np
from jax import lax
from jax.experimental import pallas as pl
from jax.experimental.pallas import tpu as pltpu
from jax.sharding import PartitionSpec as P

E = 33


def from_behind(value, axis, steps):
    count = lax.axis_size(axis)
    pairs = [(source, (source + steps) % count) for source in range(count)]
    return lax.ppermute(value, axis, pairs)


def contract(form, left, right):
    return jnp.einsum(form, left, right, precision=lax.Precision.HIGHEST)


def position_features(length):
    position_ids = jnp.arange(length, dtype=jnp.int32)
    band_count = (E - 1) // 2
    band_index = jnp.arange(1, band_count + 1, dtype=jnp.int32)
    turn_ids = band_index[:, None] * band_index[:, None] * position_ids[None, :] % length
    angles = 2.0 * math.pi / length * turn_ids.astype(jnp.float32)
    position_ramp = position_ids.astype(jnp.float32)[None, :] / length
    return jnp.concatenate([position_ramp, jnp.cos(angles), jnp.sin(angles)], axis=0)


def build_tables(length):
    fft_total = 2 * length
    outer_len = 128
    half_len = outer_len // 2
    kept_len = half_len + 1
    inner_len = fft_total // outer_len
    index_kept = jnp.arange(kept_len, dtype=jnp.int32)
    index_half = jnp.arange(half_len, dtype=jnp.int32)
    index_inner = jnp.arange(inner_len, dtype=jnp.int32)
    angle_outer = (
        2.0
        * math.pi
        / outer_len
        * (index_kept[:, None] * index_half[None, :] % outer_len).astype(jnp.float32)
    )
    cos_outer = jnp.cos(angle_outer)
    sin_outer = jnp.sin(angle_outer)
    table_first = jnp.concatenate([cos_outer, -sin_outer], axis=0)
    angle_twist = (
        2.0
        * math.pi
        / fft_total
        * (index_kept[:, None] * index_inner[None, :] % fft_total).astype(jnp.float32)
    )
    cos_twist = jnp.cos(angle_twist)[:, :, None]
    sin_twist = jnp.sin(angle_twist)[:, :, None]
    angle_inner = (
        2.0
        * math.pi
        / inner_len
        * (index_inner[:, None] * index_inner[None, :] % inner_len).astype(jnp.float32)
    )
    cos_inner = jnp.cos(angle_inner)
    sin_inner = jnp.sin(angle_inner)
    table_second = jnp.stack(
        [jnp.stack([cos_inner, sin_inner], axis=1), jnp.stack([-sin_inner, cos_inner], axis=1)],
        axis=0,
    )
    table_back = jnp.stack(
        [jnp.stack([cos_inner, -sin_inner], axis=1), jnp.stack([sin_inner, cos_inner], axis=1)],
        axis=0,
    )
    weight_kept = (
        jnp.where((index_kept == 0) | (index_kept == half_len), 1.0, 2.0).astype(jnp.float32)
        / fft_total
    )
    table_last = jnp.stack(
        [
            jnp.transpose(cos_outer) * weight_kept[None, :],
            -jnp.transpose(sin_outer) * weight_kept[None, :],
        ],
        axis=1,
    )
    return (
        table_first,
        cos_twist,
        sin_twist,
        table_second,
        table_back,
        table_last,
        half_len,
        kept_len,
        inner_len,
    )


def staged_forward(field, tables_all):
    (
        table_first,
        cos_twist,
        sin_twist,
        table_second,
        table_back,
        table_last,
        half_len,
        kept_len,
        inner_len,
    ) = tables_all
    columns = field.shape[1]
    shaped = field.reshape(half_len, inner_len, columns)
    stacked = contract("kn,npc->kpc", table_first, shaped)
    part_re = stacked[:kept_len]
    part_im = stacked[kept_len:]
    twisted = jnp.stack(
        [part_re * cos_twist + part_im * sin_twist, part_im * cos_twist - part_re * sin_twist],
        axis=0,
    )
    return contract("sqrp,rkpc->skqc", table_second, twisted)


def staged_inverse(spec, tables_all):
    (
        table_first,
        cos_twist,
        sin_twist,
        table_second,
        table_back,
        table_last,
        half_len,
        kept_len,
        inner_len,
    ) = tables_all
    columns = spec.shape[3]
    sectioned = contract("sprq,rkqc->skpc", table_back, spec)
    section_re = sectioned[0]
    section_im = sectioned[1]
    twisted = jnp.stack(
        [
            section_re * cos_twist - section_im * sin_twist,
            section_im * cos_twist + section_re * sin_twist,
        ],
        axis=0,
    )
    result = contract("nrk,rkpc->npc", table_last, twisted)
    return result.reshape(half_len * inner_len, columns)


ROWS = 128
LEVEL = 2 * ROWS
PADDED = 40
LEVELS = 4
CW = 256
AHEAD = 3
TILE = 16


def level_tables():
    odd = 2 * np.arange(LEVEL) + 1
    shift = np.arange(-LEVEL, LEVEL)
    unit = math.pi / (2 * LEVEL)
    angle = unit * ((odd[:, None] * shift[None]) % (4 * LEVEL))
    ahead = np.concatenate([np.cos(angle), -np.sin(angle)], axis=0)
    back = ahead.T / LEVEL
    back = np.concatenate([back[LEVEL:], back[:LEVEL]], axis=1)
    return jnp.asarray(ahead, jnp.bfloat16), jnp.asarray(back, jnp.bfloat16)


def padded_features(length):
    position = np.arange(length)
    band = np.arange(1, (E - 1) // 2 + 1)
    angle = 2.0 * math.pi / length * ((band[:, None] ** 2 * position[None]) % length)
    table = np.zeros((PADDED, length), np.float32)
    table[0] = position / length
    table[1 : 1 + len(band)] = np.cos(angle)
    table[1 + len(band) : E] = np.sin(angle)
    table[E] = 1.0
    return table


def section_kernel(
    pipes, per,
    v_in, g1_in, og_in, g2_in, feat_in, feat_t_in, ahead_in, back_in,
    wf, decay, skip, w_embed, bias,
    o_next, o_val, o_first, o_second, o_emb, o_wf, o_decay, o_skip,
    ins, feat, feat_t, ahead, back, ahead_k, back_g, wext, act, act_t, cos_t,
    wf_all, row_all, lev, ysend, near1, far1, far2, cin, cout, olev, landed,
    stage, fpart, kb, env, kap, spec, prod, corr, graw, gact,
    keep, sums_out, relayed, sums_in, part, parts,
    loaded, y_s, y_r, z_s, z_r, c_s, c_r, h_s, h_r, p_s, p_r,
    wf_s, wf_r, row_s, row_r, k_s, k_r, q_r, x_s, x_r,
):
    f32, bf16 = jnp.float32, jnp.bfloat16
    length = LEVELS * LEVEL
    width = wf.shape[1]
    hidden = wf.shape[0]
    shards = 2 * LEVELS
    steps = LEVELS * per
    pipe = lax.axis_index("pipe")
    me = lax.axis_index("seq")
    z, y = me // 2, me % 2
    twin = 1 - y
    partner = 2 * z + twin
    near = z // 2
    far = 1 - near
    adjacent = z + 1 - 2 * (z % 2)
    inner = (z == 1) | (z == 2)
    outer = (z == 0) | (z == 3)
    nxt = (pipe + 1) % pipes
    prv = (pipe + pipes - 1) % pipes
    high = lax.Precision.HIGHEST
    sign = (1 - 2 * near).astype(f32)

    def rows(index):
        return pl.ds(pl.multiple_of(index * ROWS, ROWS), ROWS)

    def cols(step, lane):
        block = (2 * (step // per) + lane) * per + step % per
        return pl.ds(pl.multiple_of(block * CW, CW), CW)

    def sub(step):
        return pl.ds(pl.multiple_of((step % per) * CW, CW), CW)

    def remote(src, dst, send, recv, there):
        return pltpu.make_async_remote_copy(
            src_ref=src, dst_ref=dst, send_sem=send, recv_sem=recv, device_id=there,
            device_id_type=pl.DeviceIdType.MESH,
        )

    def at_level(level):
        return (pipe, 2 * level + y)

    def crossing(kind, step):
        return remote(
            ysend.at[kind, step], lev.at[kind, step, rows(y), :],
            y_s, y_r.at[kind, step], (pipe, partner),
        )

    def crossed(kind, step):
        return remote(
            ysend.at[kind, step], lev.at[kind, step, rows(twin), :],
            y_s, y_r.at[kind, step], (pipe, partner),
        )

    def upward(slot, step, buffer, level, send):
        return remote(
            lev.at[near, step], buffer.at[step], z_s.at[send], z_r.at[slot, step],
            at_level(level),
        )

    def given(step):
        return remote(
            cout.at[step], cin.at[step], c_s, c_r.at[step], at_level(adjacent)
        )

    def homeward(kind, step):
        return remote(
            olev.at[kind, step, rows(twin), :], landed.at[kind, step], h_s, h_r.at[kind, step],
            (pipe, partner),
        )

    def handed(kind, side, step):
        out = (o_next, o_second, o_val, o_first)[kind]
        lane = (y, twin)[side]
        return remote(
            stage.at[kind, side, step], out.at[:, cols(step, lane)],
            p_s.at[kind], p_r.at[kind], (prv if kind else nxt, me),
        )

    def filters(there, source):
        return (
            remote(wf_all.at[source], wf_all.at[source], wf_s, wf_r.at[source],
                   at_level(there)),
            remote(row_all.at[source], row_all.at[source], row_s, row_r.at[source],
                   at_level(there)),
        )

    def relay(step):
        return remote(
            sums_out.at[step], relayed.at[step], k_s, q_r.at[step], at_level(adjacent)
        )

    def owed(step, slot, level):
        return remote(
            sums_out.at[step], sums_in.at[slot, step % per], k_s,
            k_r.at[slot, step % per], at_level(level),
        )

    def shared(there, source):
        return remote(part, parts.at[source], x_s, x_r, (pipe, there))

    def other_levels(visit):
        def body(step, carry):
            visit((z + 1 + step) % LEVELS)
            return carry

        lax.fori_loop(0, LEVELS - 1, body, 0)

    def others(visit):
        def body(step, carry):
            visit((me + 1 + step) % shards)
            return carry

        lax.fori_loop(0, shards - 1, body, 0)

    def every(visit):
        def body(step, carry):
            visit(step)
            return carry

        lax.fori_loop(0, steps, body, 0)

    loads = [
        pltpu.make_async_copy(src, dst, loaded.at[index])
        for index, (src, dst) in enumerate((
            (v_in, ins.at[0]), (g1_in, ins.at[1]), (og_in, ins.at[2]), (g2_in, ins.at[3]),
            (feat_in, feat), (feat_t_in, feat_t), (ahead_in, ahead), (back_in, back),
        ))
    ]
    for load in loads:
        load.start()
    barrier = pltpu.get_barrier_semaphore()

    def greet(there):
        pl.semaphore_signal(
            barrier, inc=1, device_id=(pipe, there), device_id_type=pl.DeviceIdType.MESH
        )

    others(greet)
    for beside in (nxt, prv):
        pl.semaphore_signal(
            barrier, inc=1, device_id=(beside, me), device_id_type=pl.DeviceIdType.MESH
        )
    wf_all[z] = wf[...].astype(bf16)
    row_all[z, 0:1, :] = decay[...]
    row_all[z, 1:2, :] = skip[...]
    wext[...] = jnp.zeros_like(wext)
    wext[:E, :hidden] = w_embed[:, 0, :]
    wext[:E, hidden:] = w_embed[:, 0, :]
    wext[E : E + 1, :hidden] = bias[...]
    wext[E : E + 1, hidden:] = bias[...]
    kb[:LEVEL, :] = jnp.zeros((LEVEL, CW), bf16)
    gact[...] = jnp.zeros_like(gact)
    for load in loads[:4]:
        load.wait()

    def times(kind, here):
        left, right = ins[2 * kind, :, here], ins[2 * kind + 1, :, here]
        return (left.astype(f32) * right.astype(f32)).astype(bf16)

    def weigh(step):
        for kind in (0, 1):
            ysend[kind, step] = times(kind, cols(step, twin))
            lev[kind, step, rows(y), :] = times(kind, cols(step, y))

    weigh(0)
    pl.semaphore_wait(barrier, shards + 1)

    def send_filters(there):
        for copy in filters(there, z):
            copy.start()

    def cross(step):
        crossing(near, step).start()
        crossing(far, step).start()

    cross(0)
    other_levels(send_filters)

    def weigh_and_cross(step, carry):
        weigh(step)
        cross(step)
        return carry

    lax.fori_loop(1, steps, weigh_and_cross, 0)

    def climb(step):
        crossed(near, step).wait_recv()

        @pl.when(inner)
        def _():
            upward(1, step, far1, 3 - z, 0).start()

        @pl.when(outer)
        def _():
            upward(0, step, near1, adjacent, 0).start()
            upward(2, step, far2, 3 - adjacent, 1).start()

    climb(0)
    for load in loads[4:]:
        load.wait()
    ahead_k[:LEVEL, :] = ahead[:LEVEL, :]
    ahead_k[LEVEL:, :] = (ahead[LEVEL:, :].astype(f32) * sign).astype(bf16)
    for block in range(4):
        here = slice(block * LEVEL, (block + 1) * LEVEL)
        flip = sign if block % 2 else 1.0
        back_g[:, here] = (back[:, here].astype(f32) * flip).astype(bf16)

    def activate(block, carry):
        here = pl.ds(pl.multiple_of(block * LEVEL, LEVEL), LEVEL)
        lane = lax.broadcasted_iota(jnp.int32, (LEVEL, 2 * hidden), 1)
        value = jnp.sin(jnp.dot(feat_t[here, :], wext[...], precision=high))
        top = value.astype(bf16).astype(f32)
        act[here, :] = jnp.where(lane < hidden, top, value - top).astype(bf16)
        line = lax.broadcasted_iota(jnp.int32, (2 * hidden, LEVEL), 0)
        preact = lax.dot_general(
            wext[...], feat[:, here], (((0,), (0,)), ((), ())), precision=high
        )
        value = jnp.sin(preact)
        top = value.astype(bf16).astype(f32)
        act_t[:, here] = jnp.where(line < hidden, top, value - top).astype(bf16)
        cos_t[:, here] = jnp.cos(preact[:hidden])
        return carry

    lax.fori_loop(0, LEVELS, activate, 0)
    for step in range(1, AHEAD):
        climb(step)

    def land_filters(there):
        for copy in filters(there, there):
            copy.wait_recv()

    other_levels(land_filters)

    def filter_rows(step):
        return wf_all[step // per, :, sub(step)]

    def prepare(step, depth):
        weights = filter_rows(step)
        weights = jnp.concatenate([weights, weights], axis=0)
        rate = row_all[step // per, 0:1, sub(step)]
        fine = lax.broadcasted_iota(jnp.int32, (LEVEL, 1), 0).astype(f32)
        base = jnp.exp(-rate * fine / length) * (1.0 / math.sqrt(length))
        for block in range(depth):
            here = slice(block * LEVEL, (block + 1) * LEVEL)
            raw = jnp.dot(act[here, :], weights, preferred_element_type=f32)
            envelope = base * jnp.exp(rate * (-block * LEVEL / length)) if block else base
            env[here, :] = envelope
            kb[(block + 1) * LEVEL : (block + 2) * LEVEL, :] = (raw * envelope).astype(bf16)
        kap[0] = jnp.dot(
            ahead_k[:, LEVEL:], kb[LEVEL : 2 * LEVEL, :], preferred_element_type=f32
        )
        for block in range(1, depth):
            kap[block] = jnp.dot(
                ahead_k[...], kb[block * LEVEL : (block + 2) * LEVEL, :],
                preferred_element_type=f32,
            )

    def transform(slot, source):
        spec[slot] = jnp.dot(ahead[:, LEVEL:], source, preferred_element_type=f32)

    def inverse(slot):
        return jnp.dot(back[:, : 2 * LEVEL], prod[slot], preferred_element_type=f32)

    def forth(one, two):
        return one[0] * two[0] - one[1] * two[1], one[0] * two[1] + one[1] * two[0]

    def conj(one, two):
        return one[0] * two[0] + one[1] * two[1], one[0] * two[1] - one[1] * two[0]

    def add(*terms):
        total = terms[0]
        for term in terms[1:]:
            total = total[0] + term[0], total[1] + term[1]
        return total

    def half(one):
        return one[0] * 0.5, one[1] * 0.5

    def combine(visit):
        def body(tile, carry):
            top = pl.ds(pl.multiple_of(tile * TILE, TILE), TILE)
            low = pl.ds(pl.multiple_of(LEVEL + tile * TILE, TILE), TILE)

            def read(ref, index):
                return ref[index, top, :], ref[index, low, :]

            def write(ref, index, value):
                ref[index, top, :] = value[0].astype(bf16)
                ref[index, low, :] = value[1].astype(bf16)

            visit(read, write)
            return carry

        lax.fori_loop(0, LEVEL // TILE, body, 0)

    def combine_given(read, write):
        k1, k2, k3 = [read(kap, index) for index in range(1, 4)]
        f0, f1, f2 = [read(spec, index) for index in range(2, 5)]
        write(prod, 0, add(conj(k1, f0), conj(k2, f1), conj(k3, f2)))

    def combine_inner(read, write):
        k0, k1, k2 = [read(kap, index) for index in range(3)]
        n0, n1, f0, f1, f2 = [read(spec, index) for index in range(5)]
        write(prod, 1, add(forth(k0, n0), forth(k1, n1)))
        write(prod, 2, add(conj(k0, f0), conj(k1, f1), conj(k2, f2)))
        write(corr, 0, conj(n0, f0))
        write(corr, 1, add(conj(n1, f0), conj(n0, half(f1))))
        write(corr, 2, conj(n0, f2))
        write(corr, 3, conj(half(n1), f2))

    def combine_outer(read, write):
        k0, n0, f0 = read(kap, 0), read(spec, 0), read(spec, 2)
        write(prod, 1, forth(k0, n0))
        write(prod, 2, conj(k0, f0))
        write(corr, 0, conj(n0, f0))

    def skipped(kind, step):
        return row_all[step // per, 1:2, sub(step)] * lev[kind, step].astype(f32)

    def pass_on(kind, side, step):
        lane = (y, twin)[side]
        block = (olev[kind, step, rows(y), :] if side == 0 else landed[kind, step]).astype(f32)
        here = cols(step, lane)
        for way, source in ((0, 3), (1, 2)) if kind == 0 else ((2, 1), (3, 0)):
            stage[way, side, step] = (ins[source, :, here].astype(f32) * block).astype(bf16)
            handed(way, side, step).start()

    def send_out(kind, step):
        homeward(kind, step).start()
        pass_on(kind, 0, step)

    def land(step):
        for kind in (0, 1):
            homeward(kind, step).wait_recv()
            pass_on(kind, 1, step)

    def correlate(step, depth):
        fine = lax.broadcasted_iota(jnp.int32, (LEVEL, 1), 0).astype(f32)
        total = jnp.zeros((1, CW), f32)
        for block in range(depth):
            here = slice(block * LEVEL, (block + 1) * LEVEL)
            grad = jnp.dot(back_g[:, : 2 * LEVEL], corr[block], preferred_element_type=f32)
            if block + 1 < depth:
                grad += jnp.dot(
                    back_g[:, 2 * LEVEL :], corr[block + 1], preferred_element_type=f32
                )
            graw[here, :] = (grad * env[here, :]).astype(bf16)
            kernel = kb[(block + 1) * LEVEL : (block + 2) * LEVEL, :].astype(f32)
            place = (fine + block * LEVEL) * (-1.0 / length)
            total += jnp.sum(grad * kernel * place, axis=0, keepdims=True)
        both = lev[0, step].astype(f32) * lev[1, step].astype(f32)
        skip_sum = jnp.sum(both, axis=0, keepdims=True)
        span = depth * LEVEL
        both = jnp.dot(act_t[:, :span], graw[:span, :], preferred_element_type=f32)
        share = both[:hidden] + both[hidden:]
        gact[:, :span] += lax.dot_general(
            filter_rows(step), graw[:span, :], (((1,), (1,)), ((), ())),
            preferred_element_type=f32,
        )
        keep[step, :hidden, :] = share
        keep[step, hidden : hidden + 2, :] = jnp.concatenate([total, skip_sum], axis=0)
        owner = step // per

        @pl.when(owner == adjacent)
        def _():
            pack(step, keep[step])
            owed(step, 0, adjacent).start()

        @pl.when(outer & (owner // 2 != near))
        def _():
            pack(step, keep[step])
            relay(step).start()

    def pack(step, value):
        pair = value[hidden : hidden + 2]
        top = pair.astype(bf16).astype(f32)
        tail = jnp.concatenate([top, pair - top, jnp.zeros((12, CW), f32)], axis=0)
        sums_out[step] = jnp.concatenate([value[:hidden], tail], axis=0).astype(bf16)

    def unpack(ref, *index):
        value = ref[index].astype(f32)
        tail = value[hidden:]
        return value[:hidden], tail[0:2] + tail[2:4]

    def pay(step):
        @pl.when((step // per) // 2 != near)
        def _():
            relay(step).wait_recv()
            value, pair = unpack(relayed, step)
            keep[step, :hidden, :] += value
            keep[step, hidden : hidden + 2, :] += pair
            pack(step, keep[step])
            owed(step, 1, step // per).start()

    def climb_later(step):
        @pl.when(step + AHEAD < steps)
        def _():
            climb(step + AHEAD)

    def reduce_embed():
        grad_pre = gact[...] * cos_t[...]
        part[...] = lax.dot_general(
            feat[...], jnp.concatenate([grad_pre, jnp.zeros_like(grad_pre)], axis=0),
            (((1,), (1,)), ((), ())), precision=high,
        )
        others(lambda there: shared(there, me).start())
        parts[me] = part[...]

    @pl.when(inner)
    def _():
        def turn(step):
            climb_later(step)
            prepare(step, LEVELS)
            transform(0, lev[near, step])
            crossed(far, step).wait_recv()
            transform(2, lev[far, step])
            upward(0, step, near1, adjacent, 0).wait_recv()
            transform(1, near1[step])
            upward(1, step, far1, 3 - z, 0).wait_recv()
            transform(3, far1[step])
            upward(2, step, far2, 3 - adjacent, 0).wait_recv()
            transform(4, far2[step])
            combine(combine_given)
            cout[step] = inverse(0).astype(bf16)
            given(step).start()
            combine(combine_inner)
            olev[near, step] = (inverse(1) + skipped(near, step)).astype(bf16)
            olev[far, step] = (inverse(2) + skipped(far, step)).astype(bf16)
            send_out(0, step)
            send_out(1, step)

            @pl.when(step == steps - 1)
            def _():
                lax.fori_loop(0, steps - 1, lambda early, c: (pay(early), c)[1], 0)

            correlate(step, LEVELS)

            @pl.when(step >= 1)
            def _():
                land(step - 1)

        every(turn)
        pay(steps - 1)
        reduce_embed()
        land(steps - 1)

    @pl.when(outer)
    def _():
        def settle(step):
            given(step).wait_recv()
            olev[far, step] = (fpart[step % 2] + cin[step].astype(f32)).astype(bf16)

            @pl.when(near == 0)
            def _():
                send_out(1, step)

            @pl.when(near == 1)
            def _():
                send_out(0, step)

        def turn(step):
            climb_later(step)
            prepare(step, 1)
            transform(0, lev[near, step])
            crossed(far, step).wait_recv()
            transform(2, lev[far, step])
            combine(combine_outer)
            olev[near, step] = (inverse(1) + skipped(near, step)).astype(bf16)

            @pl.when(near == 0)
            def _():
                send_out(0, step)

            @pl.when(near == 1)
            def _():
                send_out(1, step)

            fpart[step % 2] = inverse(2) + skipped(far, step)
            correlate(step, 1)

            @pl.when(step >= 1)
            def _():
                settle(step - 1)

            @pl.when(step >= 2)
            def _():
                land(step - 2)

        every(turn)
        reduce_embed()
        settle(steps - 1)
        land(steps - 2)
        land(steps - 1)

    for piece in range(per):
        here = slice(piece * CW, (piece + 1) * CW)
        step = z * per + piece
        value, pair = keep[step, :hidden, :], keep[step, hidden : hidden + 2, :]
        for slot in range(2):
            owed(step, slot, z).wait_recv()
            more, more_pair = unpack(sums_in, slot, piece)
            value, pair = value + more, pair + more_pair
        o_wf[:, here] = value
        o_decay[:, here] = pair[0:1]
        o_skip[:, here] = pair[1:2]

    remote(part, parts.at[: shards - 1], x_s, x_r, (pipe, partner)).wait_recv()
    total = parts[0]
    for index in range(1, shards):
        total = total + parts[index]
    o_emb[...] = total

    def all_sent(source, sem):
        remote(source, source, sem, sem, (pipe, partner)).wait_send()

    all_sent(wf_all.at[: LEVELS - 1], wf_s)
    all_sent(row_all.at[: LEVELS - 1], row_s)
    all_sent(ysend, y_s)
    all_sent(landed, h_s)
    all_sent(sums_out.at[: steps - per], k_s)
    all_sent(parts.at[: shards - 1], x_s)
    for kind, out in enumerate((o_next, o_second, o_val, o_first)):
        all_sent(stage.at[kind], p_s.at[kind])
        remote(out, out, p_s.at[kind], p_r.at[kind], (pipe, partner)).wait_recv()
    all_sent(far1, z_s.at[0])

    @pl.when(inner)
    def _():
        all_sent(cout, c_s)

    @pl.when(outer)
    def _():
        all_sent(far1, z_s.at[1])


VMEM_MAIN = 58 * 1024 * 1024
VMEM_FINISH = 8 * 1024 * 1024


def finish_kernel(
    a_in, b_in, c_in, d_in, emb, wf, row_d, row_s,
    a_out, b_out, c_out, d_out, o_emb, o_bias, o_wf, o_d, o_s, put,
):
    writes = [
        pltpu.make_async_copy(src, dst.at[0], put.at[kind])
        for kind, (src, dst) in enumerate(
            ((a_in, a_out), (b_in, b_out), (c_in, c_out), (d_in, d_out))
        )
    ]
    for write in writes:
        write.start()
    o_emb[:, 0, :] = emb[:E, : o_emb.shape[2]]
    o_bias[...] = emb[E : E + 1, : o_bias.shape[1]]
    o_wf[0] = wf[...]
    o_d[...] = row_d[...]
    o_s[...] = row_s[...]
    for write in writes:
        write.wait()


def fused_section(v, g1, g2, og, w_embed, b_embed, wf, decay, skip):
    pipes = lax.axis_size("pipe")
    shards = 2 * LEVELS
    length = LEVELS * LEVEL
    wide_cols = v.shape[1]
    hidden, width = wf.shape
    per = width // CW
    steps = LEVELS * per
    f32, bf16 = jnp.float32, jnp.bfloat16
    feat = padded_features(length)
    ahead, back = level_tables()
    vmem = pl.BlockSpec(memory_space=pltpu.VMEM)
    hbm = pl.BlockSpec(memory_space=pl.ANY)
    stream = pltpu.VMEM((ROWS, wide_cols), bf16)
    row = jax.ShapeDtypeStruct((1, width), f32)
    dma = pltpu.SemaphoreType.DMA
    level = pltpu.VMEM((steps, LEVEL, CW), bf16)
    results = pl.pallas_call(
        functools.partial(section_kernel, pipes, per),
        out_shape=(
            stream, stream, stream, stream,
            pltpu.VMEM((PADDED, 2 * hidden), f32),
            pltpu.VMEM((hidden, width), f32), pltpu.VMEM((1, width), f32),
            pltpu.VMEM((1, width), f32),
        ),
        in_specs=[hbm] * 8 + [vmem] * 5,
        out_specs=(vmem,) * 8,
        scratch_shapes=[
            pltpu.VMEM((4, ROWS, wide_cols), bf16),
            pltpu.VMEM((PADDED, length), f32),
            pltpu.VMEM((length, PADDED), f32),
            pltpu.VMEM((2 * LEVEL, 2 * LEVEL), bf16),
            pltpu.VMEM((LEVEL, 4 * LEVEL), bf16),
            pltpu.VMEM((2 * LEVEL, 2 * LEVEL), bf16),
            pltpu.VMEM((LEVEL, 4 * LEVEL), bf16),
            pltpu.VMEM((PADDED, 2 * hidden), f32),
            pltpu.VMEM((length, 2 * hidden), bf16),
            pltpu.VMEM((2 * hidden, length), bf16),
            pltpu.VMEM((hidden, length), f32),
            pltpu.VMEM((LEVELS, hidden, width), bf16),
            pltpu.VMEM((LEVELS, 8, width), f32),
            pltpu.VMEM((2, steps, LEVEL, CW), bf16),
            pltpu.VMEM((2, steps, ROWS, CW), bf16),
            level, level, level, level, level,
            pltpu.VMEM((2, steps, LEVEL, CW), bf16),
            pltpu.VMEM((2, steps, ROWS, CW), bf16),
            pltpu.VMEM((4, 2, steps, ROWS, CW), bf16),
            pltpu.VMEM((2, LEVEL, CW), f32),
            pltpu.VMEM((length + LEVEL, CW), bf16),
            pltpu.VMEM((length, CW), f32),
            pltpu.VMEM((LEVELS, 2 * LEVEL, CW), f32),
            pltpu.VMEM((5, 2 * LEVEL, CW), f32),
            pltpu.VMEM((3, 2 * LEVEL, CW), bf16),
            pltpu.VMEM((LEVELS, 2 * LEVEL, CW), bf16),
            pltpu.VMEM((length, CW), bf16),
            pltpu.VMEM((hidden, length), f32),
            pltpu.VMEM((steps, hidden + 8, CW), f32),
            pltpu.VMEM((steps, hidden + 16, CW), bf16),
            pltpu.VMEM((steps, hidden + 16, CW), bf16),
            pltpu.VMEM((2, per, hidden + 16, CW), bf16),
            pltpu.VMEM((PADDED, 2 * hidden), f32),
            pltpu.VMEM((shards, PADDED, 2 * hidden), f32),
            dma((8,)),
            dma, dma((2, steps)),
            dma((2,)), dma((3, steps)),
            dma, dma((steps,)),
            dma, dma((2, steps)),
            dma((4,)), dma((4,)),
            dma, dma((LEVELS,)),
            dma, dma((LEVELS,)),
            dma, dma((2, per)), dma((steps,)),
            dma, dma,
        ],
        compiler_params=pltpu.CompilerParams(
            collective_id=0, has_side_effects=True, vmem_limit_bytes=VMEM_MAIN
        ),
    )(
        v, g1, og, g2, jnp.asarray(feat), jnp.asarray(feat.T.copy()), ahead, back,
        wf, decay[None], skip[None], w_embed[:, None, :], b_embed[None],
    )
    results = [pltpu.with_memory_space_constraint(result, pltpu.VMEM) for result in results]
    final = jax.ShapeDtypeStruct((1, ROWS, wide_cols), bf16)
    done = pl.pallas_call(
        finish_kernel,
        out_shape=(
            final, final, final, final,
            jax.ShapeDtypeStruct((E, 1, hidden), f32),
            jax.ShapeDtypeStruct((1, hidden), f32),
            jax.ShapeDtypeStruct((1, hidden, width), f32), row, row,
        ),
        in_specs=[hbm] * 4 + [vmem] * 4,
        out_specs=(hbm,) * 4 + (vmem,) * 5,
        scratch_shapes=[dma((4,))],
        compiler_params=pltpu.CompilerParams(vmem_limit_bytes=VMEM_FINISH),
    )(*results)
    return done[:4] + (jnp.swapaxes(done[4], 0, 1),) + done[5:]


def spectral_product(left, right, conjugate_left):
    left_re = left[0]
    left_im = left[1]
    right_re = right[0]
    right_im = right[1]
    if conjugate_left:
        left_im = -left_im
    return jnp.stack(
        [left_re * right_re - left_im * right_im, left_re * right_im + left_im * right_re], axis=0
    )


def per_device(value_in, gate_one, gate_two, out_grad, w_embed, b_embed, w_filter, decay, skip):
    values = value_in[0]
    gate_first = gate_one[0]
    gate_second = gate_two[0]
    cotangent = out_grad[0]
    filter_w = w_filter[0]
    shards = lax.axis_size("seq")
    length = values.shape[0] * shards
    fits = length == 1024 and values.shape == (ROWS, 4096) and shards == 8
    if fits and lax.axis_size("pipe") > 2:
        return fused_section(
            values, gate_first, gate_second, cotangent,
            w_embed[0], b_embed[0], filter_w, decay[0], skip[0],
        )
    weighted = (values.astype(jnp.float32) * gate_first.astype(jnp.float32)).astype(jnp.bfloat16)
    upstream = (cotangent.astype(jnp.float32) * gate_second.astype(jnp.float32)).astype(
        jnp.bfloat16
    )
    features = position_features(length)
    preact = contract("ef,et->ft", w_embed[0], features) + b_embed[0][:, None]
    activation = jnp.sin(preact)
    positions = jnp.arange(length, dtype=jnp.int32).astype(jnp.float32)[:, None]
    envelope = jnp.exp(-decay[0][None, :] * positions / length) * (1.0 / math.sqrt(length))
    kernel = contract("ft,fc->tc", activation, filter_w) * envelope
    tables_all = build_tables(length)
    forward_transform, inverse_transform = staged_forward, staged_inverse
    kernel_spec = forward_transform(kernel, tables_all)
    skip_row = skip[0][None, :]
    weighted_chan, upstream_chan = (
        lax.all_to_all(weighted, "seq", split_axis=1, concat_axis=0, tiled=True),
        lax.all_to_all(upstream, "seq", split_axis=1, concat_axis=0, tiled=True),
    )
    weighted_f = weighted_chan.astype(jnp.float32)
    weighted_spec = forward_transform(weighted_f, tables_all)
    conv = inverse_transform(spectral_product(kernel_spec, weighted_spec, False), tables_all)
    mixed_chan, weighted_f, weighted_spec = (
        (conv + skip_row * weighted_f).astype(jnp.bfloat16),
        weighted_f,
        weighted_spec,
    )
    upstream_f = upstream_chan.astype(jnp.float32)
    upstream_spec = forward_transform(upstream_f, tables_all)
    backward_conv = inverse_transform(
        spectral_product(kernel_spec, upstream_spec, True), tables_all
    )
    grad_chan = (backward_conv + skip_row * upstream_f).astype(jnp.bfloat16)
    grad_skip = jnp.sum(upstream_f * weighted_f, axis=0)
    grad_kernel = inverse_transform(
        spectral_product(weighted_spec, upstream_spec, True), tables_all
    )
    grad_chan, grad_skip, grad_kernel = (grad_chan, grad_skip, grad_kernel)
    mixed_seq, grad_weighted = (
        lax.all_to_all(mixed_chan, "seq", split_axis=0, concat_axis=1, tiled=True),
        lax.all_to_all(grad_chan, "seq", split_axis=0, concat_axis=1, tiled=True),
    )
    output = (gate_second.astype(jnp.float32) * mixed_seq.astype(jnp.float32)).astype(jnp.bfloat16)
    next_input = from_behind(output, "pipe", 1)
    grad_decay = jnp.sum(grad_kernel * kernel * (-positions / length), axis=0)
    grad_raw = grad_kernel * envelope
    grad_filter_w = contract("ft,tc->fc", activation, grad_raw)
    grad_preact = contract("fc,tc->ft", filter_w, grad_raw) * jnp.cos(preact)
    part_weight = contract("et,ft->ef", features, grad_preact)
    part_bias = jnp.sum(grad_preact, axis=1)
    grad_embed_w, grad_embed_b = lax.psum((part_weight, part_bias), "seq")
    grad_values = (grad_weighted.astype(jnp.float32) * gate_first.astype(jnp.float32)).astype(
        jnp.bfloat16
    )
    grad_first = (grad_weighted.astype(jnp.float32) * values.astype(jnp.float32)).astype(
        jnp.bfloat16
    )
    grad_second = (cotangent.astype(jnp.float32) * mixed_seq.astype(jnp.float32)).astype(
        jnp.bfloat16
    )
    moved_values, moved_first, moved_second = from_behind(
        (grad_values, grad_first, grad_second), "pipe", -1
    )
    return (
        next_input[None],
        moved_values[None],
        moved_first[None],
        moved_second[None],
        grad_embed_w[None],
        grad_embed_b[None],
        grad_filter_w[None],
        grad_decay[None],
        grad_skip[None],
    )


def solution(mesh):
    return jax.shard_map(
        per_device,
        mesh=mesh,
        in_specs=(
            P("pipe", "seq", None),
            P("pipe", "seq", None),
            P("pipe", "seq", None),
            P("pipe", "seq", None),
            P("pipe", None, None),
            P("pipe", None),
            P("pipe", None, "seq"),
            P("pipe", "seq"),
            P("pipe", "seq"),
        ),
        out_specs=(
            P("pipe", "seq", None),
            P("pipe", "seq", None),
            P("pipe", "seq", None),
            P("pipe", "seq", None),
            P("pipe", None, None),
            P("pipe", None),
            P("pipe", None, "seq"),
            P("pipe", "seq"),
            P("pipe", "seq"),
        ),
        check_vma=False,
    )
```

```python
import functools
import math

import jax
import jax.numpy as jnp
import numpy as np
from jax import lax
from jax.experimental import pallas as pl
from jax.experimental.pallas import tpu as pltpu
from jax.sharding import PartitionSpec as P

E = 33


def from_behind(value, axis, steps):
    count = lax.axis_size(axis)
    pairs = [(source, (source + steps) % count) for source in range(count)]
    return lax.ppermute(value, axis, pairs)


def contract(form, left, right):
    return jnp.einsum(form, left, right, precision=lax.Precision.HIGHEST)


def position_features(length):
    position_ids = jnp.arange(length, dtype=jnp.int32)
    band_count = (E - 1) // 2
    band_index = jnp.arange(1, band_count + 1, dtype=jnp.int32)
    turn_ids = band_index[:, None] * band_index[:, None] * position_ids[None, :] % length
    angles = 2.0 * math.pi / length * turn_ids.astype(jnp.float32)
    position_ramp = position_ids.astype(jnp.float32)[None, :] / length
    return jnp.concatenate([position_ramp, jnp.cos(angles), jnp.sin(angles)], axis=0)


def build_tables(length):
    fft_total = 2 * length
    outer_len = 128
    half_len = outer_len // 2
    kept_len = half_len + 1
    inner_len = fft_total // outer_len
    index_kept = jnp.arange(kept_len, dtype=jnp.int32)
    index_half = jnp.arange(half_len, dtype=jnp.int32)
    index_inner = jnp.arange(inner_len, dtype=jnp.int32)
    angle_outer = (
        2.0
        * math.pi
        / outer_len
        * (index_kept[:, None] * index_half[None, :] % outer_len).astype(jnp.float32)
    )
    cos_outer = jnp.cos(angle_outer)
    sin_outer = jnp.sin(angle_outer)
    table_first = jnp.concatenate([cos_outer, -sin_outer], axis=0)
    angle_twist = (
        2.0
        * math.pi
        / fft_total
        * (index_kept[:, None] * index_inner[None, :] % fft_total).astype(jnp.float32)
    )
    cos_twist = jnp.cos(angle_twist)[:, :, None]
    sin_twist = jnp.sin(angle_twist)[:, :, None]
    angle_inner = (
        2.0
        * math.pi
        / inner_len
        * (index_inner[:, None] * index_inner[None, :] % inner_len).astype(jnp.float32)
    )
    cos_inner = jnp.cos(angle_inner)
    sin_inner = jnp.sin(angle_inner)
    table_second = jnp.stack(
        [jnp.stack([cos_inner, sin_inner], axis=1), jnp.stack([-sin_inner, cos_inner], axis=1)],
        axis=0,
    )
    table_back = jnp.stack(
        [jnp.stack([cos_inner, -sin_inner], axis=1), jnp.stack([sin_inner, cos_inner], axis=1)],
        axis=0,
    )
    weight_kept = (
        jnp.where((index_kept == 0) | (index_kept == half_len), 1.0, 2.0).astype(jnp.float32)
        / fft_total
    )
    table_last = jnp.stack(
        [
            jnp.transpose(cos_outer) * weight_kept[None, :],
            -jnp.transpose(sin_outer) * weight_kept[None, :],
        ],
        axis=1,
    )
    return (
        table_first,
        cos_twist,
        sin_twist,
        table_second,
        table_back,
        table_last,
        half_len,
        kept_len,
        inner_len,
    )


def staged_forward(field, tables_all):
    (
        table_first,
        cos_twist,
        sin_twist,
        table_second,
        table_back,
        table_last,
        half_len,
        kept_len,
        inner_len,
    ) = tables_all
    columns = field.shape[1]
    shaped = field.reshape(half_len, inner_len, columns)
    stacked = contract("kn,npc->kpc", table_first, shaped)
    part_re = stacked[:kept_len]
    part_im = stacked[kept_len:]
    twisted = jnp.stack(
        [part_re * cos_twist + part_im * sin_twist, part_im * cos_twist - part_re * sin_twist],
        axis=0,
    )
    return contract("sqrp,rkpc->skqc", table_second, twisted)


def staged_inverse(spec, tables_all):
    (
        table_first,
        cos_twist,
        sin_twist,
        table_second,
        table_back,
        table_last,
        half_len,
        kept_len,
        inner_len,
    ) = tables_all
    columns = spec.shape[3]
    sectioned = contract("sprq,rkqc->skpc", table_back, spec)
    section_re = sectioned[0]
    section_im = sectioned[1]
    twisted = jnp.stack(
        [
            section_re * cos_twist - section_im * sin_twist,
            section_im * cos_twist + section_re * sin_twist,
        ],
        axis=0,
    )
    result = contract("nrk,rkpc->npc", table_last, twisted)
    return result.reshape(half_len * inner_len, columns)


ROWS = 128
LEVEL = 2 * ROWS
PADDED = 40
LEVELS = 4
CW = 256
AHEAD = 5
TILE = 16


def level_tables():
    odd = 2 * np.arange(LEVEL) + 1
    shift = np.arange(-LEVEL, LEVEL)
    unit = math.pi / (2 * LEVEL)
    angle = unit * ((odd[:, None] * shift[None]) % (4 * LEVEL))
    ahead = np.concatenate([np.cos(angle), -np.sin(angle)], axis=0)
    back = ahead.T / LEVEL
    back = np.concatenate([back[LEVEL:], back[:LEVEL]], axis=1)
    return jnp.asarray(ahead, jnp.bfloat16), jnp.asarray(back, jnp.bfloat16)


def padded_features(length):
    position = np.arange(length)
    band = np.arange(1, (E - 1) // 2 + 1)
    angle = 2.0 * math.pi / length * ((band[:, None] ** 2 * position[None]) % length)
    table = np.zeros((PADDED, length), np.float32)
    table[0] = position / length
    table[1 : 1 + len(band)] = np.cos(angle)
    table[1 + len(band) : E] = np.sin(angle)
    table[E] = 1.0
    return table


def section_kernel(
    pipes, per,
    v_in, g1_in, og_in, g2_in, feat_in, feat_t_in, ahead_in, back_in,
    wf, decay, skip, w_embed, bias,
    o_next, o_val, o_first, o_second, o_emb, o_wf, o_decay, o_skip,
    ins, feat, feat_t, ahead, back, ahead_k, back_g, wext, act, act_t, cos_t,
    wf_all, row_all, lev, ysend, near1, far1, far2, cin, cout, olev, landed,
    stage, fpart, kb, env, kap, spec, prod, corr, graw, gact,
    keep, sums_out, relayed, sums_in, part, parts,
    loaded, y_s, y_r, z_s, z_r, c_s, c_r, h_s, h_r, p_s, p_r,
    wf_s, wf_r, row_s, row_r, k_s, k_r, q_r, x_s, x_r,
):
    f32, bf16 = jnp.float32, jnp.bfloat16
    length = LEVELS * LEVEL
    width = wf.shape[1]
    hidden = wf.shape[0]
    shards = 2 * LEVELS
    steps = LEVELS * per
    pipe = lax.axis_index("pipe")
    me = lax.axis_index("seq")
    z, y = me // 2, me % 2
    twin = 1 - y
    partner = 2 * z + twin
    near = z // 2
    far = 1 - near
    adjacent = z + 1 - 2 * (z % 2)
    inner = (z == 1) | (z == 2)
    outer = (z == 0) | (z == 3)
    nxt = (pipe + 1) % pipes
    prv = (pipe + pipes - 1) % pipes
    high = lax.Precision.HIGHEST
    sign = (1 - 2 * near).astype(f32)

    def rows(index):
        return pl.ds(pl.multiple_of(index * ROWS, ROWS), ROWS)

    def cols(step, lane):
        block = (2 * (step // per) + lane) * per + step % per
        return pl.ds(pl.multiple_of(block * CW, CW), CW)

    def sub(step):
        return pl.ds(pl.multiple_of((step % per) * CW, CW), CW)

    def remote(src, dst, send, recv, there):
        return pltpu.make_async_remote_copy(
            src_ref=src, dst_ref=dst, send_sem=send, recv_sem=recv, device_id=there,
            device_id_type=pl.DeviceIdType.MESH,
        )

    def at_level(level):
        return (pipe, 2 * level + y)

    def crossing(kind, step):
        return remote(
            ysend.at[kind, step], lev.at[kind, step, rows(y), :],
            y_s, y_r.at[kind, step], (pipe, partner),
        )

    def crossed(kind, step):
        return remote(
            ysend.at[kind, step], lev.at[kind, step, rows(twin), :],
            y_s, y_r.at[kind, step], (pipe, partner),
        )

    def upward(slot, step, buffer, level, send):
        return remote(
            lev.at[near, step], buffer.at[step], z_s.at[send], z_r.at[slot, step],
            at_level(level),
        )

    def given(step):
        return remote(
            cout.at[step], cin.at[step], c_s, c_r.at[step], at_level(adjacent)
        )

    def homeward(kind, step):
        return remote(
            olev.at[kind, step, rows(twin), :], landed.at[kind, step], h_s, h_r.at[kind, step],
            (pipe, partner),
        )

    def handed(kind, side, step):
        out = (o_next, o_second, o_val, o_first)[kind]
        lane = (y, twin)[side]
        return remote(
            stage.at[kind, side, step], out.at[:, cols(step, lane)],
            p_s.at[kind], p_r.at[kind], (prv if kind else nxt, me),
        )

    def filters(there, source):
        return (
            remote(wf_all.at[source], wf_all.at[source], wf_s, wf_r.at[source],
                   at_level(there)),
            remote(row_all.at[source], row_all.at[source], row_s, row_r.at[source],
                   at_level(there)),
        )

    def relay(step):
        return remote(
            sums_out.at[step], relayed.at[step], k_s, q_r.at[step], at_level(adjacent)
        )

    def owed(step, slot, level):
        return remote(
            sums_out.at[step], sums_in.at[slot, step % per], k_s,
            k_r.at[slot, step % per], at_level(level),
        )

    def shared(there, source):
        return remote(part, parts.at[source], x_s, x_r, (pipe, there))

    def other_levels(visit):
        def body(step, carry):
            visit((z + 1 + step) % LEVELS)
            return carry

        lax.fori_loop(0, LEVELS - 1, body, 0)

    def others(visit):
        def body(step, carry):
            visit((me + 1 + step) % shards)
            return carry

        lax.fori_loop(0, shards - 1, body, 0)

    def every(visit):
        def body(step, carry):
            visit(step)
            return carry

        lax.fori_loop(0, steps, body, 0)

    loads = [
        pltpu.make_async_copy(src, dst, loaded.at[index])
        for index, (src, dst) in enumerate((
            (v_in, ins.at[0]), (g1_in, ins.at[1]), (og_in, ins.at[2]), (g2_in, ins.at[3]),
            (feat_in, feat), (feat_t_in, feat_t), (ahead_in, ahead), (back_in, back),
        ))
    ]
    for load in loads[:4]:
        load.start()
    barrier = pltpu.get_barrier_semaphore()

    def greet(there):
        pl.semaphore_signal(
            barrier, inc=1, device_id=(pipe, there), device_id_type=pl.DeviceIdType.MESH
        )

    others(greet)
    for beside in (nxt, prv):
        pl.semaphore_signal(
            barrier, inc=1, device_id=(beside, me), device_id_type=pl.DeviceIdType.MESH
        )
    wf_all[z] = wf[...].astype(bf16)
    row_all[z, 0:1, :] = decay[...]
    row_all[z, 1:2, :] = skip[...]
    def times(kind, here):
        left, right = ins[2 * kind, :, here], ins[2 * kind + 1, :, here]
        return (left.astype(f32) * right.astype(f32)).astype(bf16)

    def weigh(step):
        for kind in (0, 1):
            ysend[kind, step] = times(kind, cols(step, twin))
            lev[kind, step, rows(y), :] = times(kind, cols(step, y))

    pl.semaphore_wait(barrier, shards + 1)

    def send_filters(there):
        for copy in filters(there, z):
            copy.start()

    def cross(step):
        crossing(near, step).start()
        crossing(far, step).start()

    other_levels(send_filters)
    for load in loads[:4]:
        load.wait()
    weigh(0)
    cross(0)

    def weigh_and_cross(step, carry):
        weigh(step)
        cross(step)
        return carry

    for load in loads[4:]:
        load.start()
    lax.fori_loop(1, steps, weigh_and_cross, 0)
    wext[...] = jnp.zeros_like(wext)
    wext[:E, :hidden] = w_embed[:, 0, :]
    wext[:E, hidden:] = w_embed[:, 0, :]
    wext[E : E + 1, :hidden] = bias[...]
    wext[E : E + 1, hidden:] = bias[...]
    kb[:LEVEL, :] = jnp.zeros((LEVEL, CW), bf16)
    gact[...] = jnp.zeros_like(gact)

    def climb(step):
        crossed(near, step).wait_recv()

        @pl.when(inner)
        def _():
            upward(1, step, far1, 3 - z, 0).start()

        @pl.when(outer)
        def _():
            upward(2, step, far2, 3 - adjacent, 1).start()
            upward(0, step, near1, adjacent, 0).start()

    climb(0)
    for load in loads[4:]:
        load.wait()
    ahead_k[:LEVEL, :] = ahead[:LEVEL, :]
    ahead_k[LEVEL:, :] = (ahead[LEVEL:, :].astype(f32) * sign).astype(bf16)
    for block in range(4):
        here = slice(block * LEVEL, (block + 1) * LEVEL)
        flip = sign if block % 2 else 1.0
        back_g[:, here] = (back[:, here].astype(f32) * flip).astype(bf16)

    def activate(block, carry):
        here = pl.ds(pl.multiple_of(block * LEVEL, LEVEL), LEVEL)
        lane = lax.broadcasted_iota(jnp.int32, (LEVEL, 2 * hidden), 1)
        value = jnp.sin(jnp.dot(feat_t[here, :], wext[...], precision=high))
        top = value.astype(bf16).astype(f32)
        act[here, :] = jnp.where(lane < hidden, top, value - top).astype(bf16)
        line = lax.broadcasted_iota(jnp.int32, (2 * hidden, LEVEL), 0)
        preact = lax.dot_general(
            wext[...], feat[:, here], (((0,), (0,)), ((), ())), precision=high
        )
        value = jnp.sin(preact)
        top = value.astype(bf16).astype(f32)
        act_t[:, here] = jnp.where(line < hidden, top, value - top).astype(bf16)
        cos_t[:, here] = jnp.cos(preact[:hidden])
        return carry

    lax.fori_loop(0, LEVELS, activate, 0)
    for step in range(1, AHEAD):
        climb(step)

    def land_filters(there):
        for copy in filters(there, there):
            copy.wait_recv()

    other_levels(land_filters)

    def filter_rows(step):
        return wf_all[step // per, :, sub(step)]

    def prepare(step, depth):
        weights = filter_rows(step)
        weights = jnp.concatenate([weights, weights], axis=0)
        rate = row_all[step // per, 0:1, sub(step)]
        fine = lax.broadcasted_iota(jnp.int32, (LEVEL, 1), 0).astype(f32)
        base = jnp.exp(-rate * fine / length) * (1.0 / math.sqrt(length))
        for block in range(depth):
            here = slice(block * LEVEL, (block + 1) * LEVEL)
            raw = jnp.dot(act[here, :], weights, preferred_element_type=f32)
            envelope = base * jnp.exp(rate * (-block * LEVEL / length)) if block else base
            env[here, :] = envelope
            kb[(block + 1) * LEVEL : (block + 2) * LEVEL, :] = (raw * envelope).astype(bf16)
        kap[0] = jnp.dot(
            ahead_k[:, LEVEL:], kb[LEVEL : 2 * LEVEL, :], preferred_element_type=f32
        )
        for block in range(1, depth):
            kap[block] = jnp.dot(
                ahead_k[...], kb[block * LEVEL : (block + 2) * LEVEL, :],
                preferred_element_type=f32,
            )

    def transform(slot, source):
        spec[slot] = jnp.dot(ahead[:, LEVEL:], source, preferred_element_type=f32)

    def inverse(slot):
        return jnp.dot(back[:, : 2 * LEVEL], prod[slot], preferred_element_type=f32)

    def forth(one, two):
        return one[0] * two[0] - one[1] * two[1], one[0] * two[1] + one[1] * two[0]

    def conj(one, two):
        return one[0] * two[0] + one[1] * two[1], one[0] * two[1] - one[1] * two[0]

    def add(*terms):
        total = terms[0]
        for term in terms[1:]:
            total = total[0] + term[0], total[1] + term[1]
        return total

    def half(one):
        return one[0] * 0.5, one[1] * 0.5

    def combine(visit):
        def body(tile, carry):
            top = pl.ds(pl.multiple_of(tile * TILE, TILE), TILE)
            low = pl.ds(pl.multiple_of(LEVEL + tile * TILE, TILE), TILE)

            def read(ref, index):
                return ref[index, top, :], ref[index, low, :]

            def write(ref, index, value):
                ref[index, top, :] = value[0].astype(bf16)
                ref[index, low, :] = value[1].astype(bf16)

            visit(read, write)
            return carry

        lax.fori_loop(0, LEVEL // TILE, body, 0, unroll=4)

    def combine_given(read, write):
        k1, k2, k3 = [read(kap, index) for index in range(1, 4)]
        f0, f1, f2 = [read(spec, index) for index in range(2, 5)]
        write(prod, 0, add(conj(k1, f0), conj(k2, f1), conj(k3, f2)))

    def combine_inner(read, write):
        k0, k1, k2 = [read(kap, index) for index in range(3)]
        n0, n1, f0, f1, f2 = [read(spec, index) for index in range(5)]
        write(prod, 1, add(forth(k0, n0), forth(k1, n1)))
        write(prod, 2, add(conj(k0, f0), conj(k1, f1), conj(k2, f2)))
        write(corr, 0, conj(n0, f0))
        write(corr, 1, add(conj(n1, f0), conj(n0, half(f1))))
        write(corr, 2, conj(n0, f2))
        write(corr, 3, conj(half(n1), f2))

    def combine_outer(read, write):
        k0, n0, f0 = read(kap, 0), read(spec, 0), read(spec, 2)
        write(prod, 1, forth(k0, n0))
        write(prod, 2, conj(k0, f0))
        write(corr, 0, conj(n0, f0))

    def skipped(kind, step):
        return row_all[step // per, 1:2, sub(step)] * lev[kind, step].astype(f32)

    def pass_on(kind, side, step):
        lane = (y, twin)[side]
        block = (olev[kind, step, rows(y), :] if side == 0 else landed[kind, step]).astype(f32)
        here = cols(step, lane)
        for way, source in ((0, 3), (1, 2)) if kind == 0 else ((2, 1), (3, 0)):
            stage[way, side, step] = (ins[source, :, here].astype(f32) * block).astype(bf16)
            handed(way, side, step).start()

    def send_out(kind, step):
        homeward(kind, step).start()
        pass_on(kind, 0, step)

    def land(step):
        for kind in (0, 1):
            homeward(kind, step).wait_recv()
            pass_on(kind, 1, step)

    def correlate(step, depth):
        fine = lax.broadcasted_iota(jnp.int32, (LEVEL, 1), 0).astype(f32)
        total = jnp.zeros((1, CW), f32)
        for block in range(depth):
            here = slice(block * LEVEL, (block + 1) * LEVEL)
            grad = jnp.dot(back_g[:, : 2 * LEVEL], corr[block], preferred_element_type=f32)
            if block + 1 < depth:
                grad += jnp.dot(
                    back_g[:, 2 * LEVEL :], corr[block + 1], preferred_element_type=f32
                )
            graw[here, :] = (grad * env[here, :]).astype(bf16)
            kernel = kb[(block + 1) * LEVEL : (block + 2) * LEVEL, :].astype(f32)
            place = (fine + block * LEVEL) * (-1.0 / length)
            total += jnp.sum(grad * kernel * place, axis=0, keepdims=True)
        both = lev[0, step].astype(f32) * lev[1, step].astype(f32)
        skip_sum = jnp.sum(both, axis=0, keepdims=True)
        span = depth * LEVEL
        both = jnp.dot(act_t[:, :span], graw[:span, :], preferred_element_type=f32)
        share = both[:hidden] + both[hidden:]
        gact[:, :span] += lax.dot_general(
            filter_rows(step), graw[:span, :], (((1,), (1,)), ((), ())),
            preferred_element_type=f32,
        )
        keep[step, :hidden, :] = share
        keep[step, hidden : hidden + 2, :] = jnp.concatenate([total, skip_sum], axis=0)
        owner = step // per

        @pl.when(owner == adjacent)
        def _():
            pack(step, keep[step])
            owed(step, 0, adjacent).start()

        @pl.when(outer & (owner // 2 != near))
        def _():
            pack(step, keep[step])
            relay(step).start()

    def pack(step, value):
        pair = value[hidden : hidden + 2]
        top = pair.astype(bf16).astype(f32)
        tail = jnp.concatenate([top, pair - top, jnp.zeros((12, CW), f32)], axis=0)
        sums_out[step] = jnp.concatenate([value[:hidden], tail], axis=0).astype(bf16)

    def unpack(ref, *index):
        value = ref[index].astype(f32)
        tail = value[hidden:]
        return value[:hidden], tail[0:2] + tail[2:4]

    def pay(step):
        @pl.when((step // per) // 2 != near)
        def _():
            relay(step).wait_recv()
            value, pair = unpack(relayed, step)
            keep[step, :hidden, :] += value
            keep[step, hidden : hidden + 2, :] += pair
            pack(step, keep[step])
            owed(step, 1, step // per).start()

    def climb_later(step):
        @pl.when(step + AHEAD < steps)
        def _():
            climb(step + AHEAD)

    def reduce_embed():
        grad_pre = gact[...] * cos_t[...]
        part[...] = lax.dot_general(
            feat[...], jnp.concatenate([grad_pre, jnp.zeros_like(grad_pre)], axis=0),
            (((1,), (1,)), ((), ())), precision=high,
        )
        others(lambda there: shared(there, me).start())
        parts[me] = part[...]

    @pl.when(inner)
    def _():
        def turn(step):
            climb_later(step)
            prepare(step, LEVELS)
            transform(0, lev[near, step])
            crossed(far, step).wait_recv()
            transform(2, lev[far, step])
            upward(0, step, near1, adjacent, 0).wait_recv()
            transform(1, near1[step])
            upward(1, step, far1, 3 - z, 0).wait_recv()
            transform(3, far1[step])
            upward(2, step, far2, 3 - adjacent, 0).wait_recv()
            transform(4, far2[step])
            combine(combine_given)
            cout[step] = inverse(0).astype(bf16)
            given(step).start()
            combine(combine_inner)
            olev[near, step] = (inverse(1) + skipped(near, step)).astype(bf16)
            olev[far, step] = (inverse(2) + skipped(far, step)).astype(bf16)
            send_out(0, step)
            send_out(1, step)

            @pl.when(step == steps - 1)
            def _():
                lax.fori_loop(0, steps - 1, lambda early, c: (pay(early), c)[1], 0)

            correlate(step, LEVELS)

            @pl.when(step >= 1)
            def _():
                land(step - 1)

        every(turn)
        pay(steps - 1)
        reduce_embed()
        land(steps - 1)

    @pl.when(outer)
    def _():
        def settle(step):
            given(step).wait_recv()
            olev[far, step] = (fpart[step % 2] + cin[step].astype(f32)).astype(bf16)

            @pl.when(near == 0)
            def _():
                send_out(1, step)

            @pl.when(near == 1)
            def _():
                send_out(0, step)

        def turn(step):
            climb_later(step)
            prepare(step, 1)
            transform(0, lev[near, step])
            crossed(far, step).wait_recv()
            transform(2, lev[far, step])
            combine(combine_outer)
            olev[near, step] = (inverse(1) + skipped(near, step)).astype(bf16)

            @pl.when(near == 0)
            def _():
                send_out(0, step)

            @pl.when(near == 1)
            def _():
                send_out(1, step)

            fpart[step % 2] = inverse(2) + skipped(far, step)
            correlate(step, 1)

            @pl.when(step >= 1)
            def _():
                settle(step - 1)

            @pl.when(step >= 2)
            def _():
                land(step - 2)

        every(turn)
        reduce_embed()
        settle(steps - 1)
        land(steps - 2)
        land(steps - 1)

    for piece in range(per):
        here = slice(piece * CW, (piece + 1) * CW)
        step = z * per + piece
        value, pair = keep[step, :hidden, :], keep[step, hidden : hidden + 2, :]
        for slot in range(2):
            owed(step, slot, z).wait_recv()
            more, more_pair = unpack(sums_in, slot, piece)
            value, pair = value + more, pair + more_pair
        o_wf[:, here] = value
        o_decay[:, here] = pair[0:1]
        o_skip[:, here] = pair[1:2]

    remote(part, parts.at[: shards - 1], x_s, x_r, (pipe, partner)).wait_recv()
    total = parts[0]
    for index in range(1, shards):
        total = total + parts[index]
    o_emb[...] = total

    def all_sent(source, sem):
        remote(source, source, sem, sem, (pipe, partner)).wait_send()

    all_sent(wf_all.at[: LEVELS - 1], wf_s)
    all_sent(row_all.at[: LEVELS - 1], row_s)
    all_sent(ysend, y_s)
    all_sent(landed, h_s)
    all_sent(sums_out.at[: steps - per], k_s)
    all_sent(parts.at[: shards - 1], x_s)
    for kind, out in enumerate((o_next, o_second, o_val, o_first)):
        all_sent(stage.at[kind], p_s.at[kind])
        remote(out, out, p_s.at[kind], p_r.at[kind], (pipe, partner)).wait_recv()
    all_sent(far1, z_s.at[0])

    @pl.when(inner)
    def _():
        all_sent(cout, c_s)

    @pl.when(outer)
    def _():
        all_sent(far1, z_s.at[1])


VMEM_MAIN = 58 * 1024 * 1024
VMEM_FINISH = 8 * 1024 * 1024


def finish_kernel(
    a_in, b_in, c_in, d_in, emb, wf, row_d, row_s,
    a_out, b_out, c_out, d_out, o_emb, o_bias, o_wf, o_d, o_s, put,
):
    writes = [
        pltpu.make_async_copy(src, dst.at[0], put.at[kind])
        for kind, (src, dst) in enumerate(
            ((a_in, a_out), (b_in, b_out), (c_in, c_out), (d_in, d_out))
        )
    ]
    for write in writes:
        write.start()
    o_emb[:, 0, :] = emb[:E, : o_emb.shape[2]]
    o_bias[...] = emb[E : E + 1, : o_bias.shape[1]]
    o_wf[0] = wf[...]
    o_d[...] = row_d[...]
    o_s[...] = row_s[...]
    for write in writes:
        write.wait()


def fused_section(v, g1, g2, og, w_embed, b_embed, wf, decay, skip):
    pipes = lax.axis_size("pipe")
    shards = 2 * LEVELS
    length = LEVELS * LEVEL
    wide_cols = v.shape[1]
    hidden, width = wf.shape
    per = width // CW
    steps = LEVELS * per
    f32, bf16 = jnp.float32, jnp.bfloat16
    feat = padded_features(length)
    ahead, back = level_tables()
    vmem = pl.BlockSpec(memory_space=pltpu.VMEM)
    hbm = pl.BlockSpec(memory_space=pl.ANY)
    stream = pltpu.VMEM((ROWS, wide_cols), bf16)
    row = jax.ShapeDtypeStruct((1, width), f32)
    dma = pltpu.SemaphoreType.DMA
    level = pltpu.VMEM((steps, LEVEL, CW), bf16)
    results = pl.pallas_call(
        functools.partial(section_kernel, pipes, per),
        out_shape=(
            stream, stream, stream, stream,
            pltpu.VMEM((PADDED, 2 * hidden), f32),
            pltpu.VMEM((hidden, width), f32), pltpu.VMEM((1, width), f32),
            pltpu.VMEM((1, width), f32),
        ),
        in_specs=[hbm] * 8 + [vmem] * 5,
        out_specs=(vmem,) * 8,
        scratch_shapes=[
            pltpu.VMEM((4, ROWS, wide_cols), bf16),
            pltpu.VMEM((PADDED, length), f32),
            pltpu.VMEM((length, PADDED), f32),
            pltpu.VMEM((2 * LEVEL, 2 * LEVEL), bf16),
            pltpu.VMEM((LEVEL, 4 * LEVEL), bf16),
            pltpu.VMEM((2 * LEVEL, 2 * LEVEL), bf16),
            pltpu.VMEM((LEVEL, 4 * LEVEL), bf16),
            pltpu.VMEM((PADDED, 2 * hidden), f32),
            pltpu.VMEM((length, 2 * hidden), bf16),
            pltpu.VMEM((2 * hidden, length), bf16),
            pltpu.VMEM((hidden, length), f32),
            pltpu.VMEM((LEVELS, hidden, width), bf16),
            pltpu.VMEM((LEVELS, 8, width), f32),
            pltpu.VMEM((2, steps, LEVEL, CW), bf16),
            pltpu.VMEM((2, steps, ROWS, CW), bf16),
            level, level, level, level, level,
            pltpu.VMEM((2, steps, LEVEL, CW), bf16),
            pltpu.VMEM((2, steps, ROWS, CW), bf16),
            pltpu.VMEM((4, 2, steps, ROWS, CW), bf16),
            pltpu.VMEM((2, LEVEL, CW), f32),
            pltpu.VMEM((length + LEVEL, CW), bf16),
            pltpu.VMEM((length, CW), f32),
            pltpu.VMEM((LEVELS, 2 * LEVEL, CW), f32),
            pltpu.VMEM((5, 2 * LEVEL, CW), f32),
            pltpu.VMEM((3, 2 * LEVEL, CW), bf16),
            pltpu.VMEM((LEVELS, 2 * LEVEL, CW), bf16),
            pltpu.VMEM((length, CW), bf16),
            pltpu.VMEM((hidden, length), f32),
            pltpu.VMEM((steps, hidden + 8, CW), f32),
            pltpu.VMEM((steps, hidden + 16, CW), bf16),
            pltpu.VMEM((steps, hidden + 16, CW), bf16),
            pltpu.VMEM((2, per, hidden + 16, CW), bf16),
            pltpu.VMEM((PADDED, 2 * hidden), f32),
            pltpu.VMEM((shards, PADDED, 2 * hidden), f32),
            dma((8,)),
            dma, dma((2, steps)),
            dma((2,)), dma((3, steps)),
            dma, dma((steps,)),
            dma, dma((2, steps)),
            dma((4,)), dma((4,)),
            dma, dma((LEVELS,)),
            dma, dma((LEVELS,)),
            dma, dma((2, per)), dma((steps,)),
            dma, dma,
        ],
        compiler_params=pltpu.CompilerParams(
            collective_id=0, has_side_effects=True, vmem_limit_bytes=VMEM_MAIN
        ),
    )(
        v, g1, og, g2, jnp.asarray(feat), jnp.asarray(feat.T.copy()), ahead, back,
        wf, decay[None], skip[None], w_embed[:, None, :], b_embed[None],
    )
    results = [pltpu.with_memory_space_constraint(result, pltpu.VMEM) for result in results]
    final = jax.ShapeDtypeStruct((1, ROWS, wide_cols), bf16)
    done = pl.pallas_call(
        finish_kernel,
        out_shape=(
            final, final, final, final,
            jax.ShapeDtypeStruct((E, 1, hidden), f32),
            jax.ShapeDtypeStruct((1, hidden), f32),
            jax.ShapeDtypeStruct((1, hidden, width), f32), row, row,
        ),
        in_specs=[hbm] * 4 + [vmem] * 4,
        out_specs=(hbm,) * 4 + (vmem,) * 5,
        scratch_shapes=[dma((4,))],
        compiler_params=pltpu.CompilerParams(vmem_limit_bytes=VMEM_FINISH),
    )(*results)
    return done[:4] + (jnp.swapaxes(done[4], 0, 1),) + done[5:]


def spectral_product(left, right, conjugate_left):
    left_re = left[0]
    left_im = left[1]
    right_re = right[0]
    right_im = right[1]
    if conjugate_left:
        left_im = -left_im
    return jnp.stack(
        [left_re * right_re - left_im * right_im, left_re * right_im + left_im * right_re], axis=0
    )


def per_device(value_in, gate_one, gate_two, out_grad, w_embed, b_embed, w_filter, decay, skip):
    values = value_in[0]
    gate_first = gate_one[0]
    gate_second = gate_two[0]
    cotangent = out_grad[0]
    filter_w = w_filter[0]
    shards = lax.axis_size("seq")
    length = values.shape[0] * shards
    fits = length == 1024 and values.shape == (ROWS, 4096) and shards == 8
    if fits and lax.axis_size("pipe") > 2:
        return fused_section(
            values, gate_first, gate_second, cotangent,
            w_embed[0], b_embed[0], filter_w, decay[0], skip[0],
        )
    weighted = (values.astype(jnp.float32) * gate_first.astype(jnp.float32)).astype(jnp.bfloat16)
    upstream = (cotangent.astype(jnp.float32) * gate_second.astype(jnp.float32)).astype(
        jnp.bfloat16
    )
    features = position_features(length)
    preact = contract("ef,et->ft", w_embed[0], features) + b_embed[0][:, None]
    activation = jnp.sin(preact)
    positions = jnp.arange(length, dtype=jnp.int32).astype(jnp.float32)[:, None]
    envelope = jnp.exp(-decay[0][None, :] * positions / length) * (1.0 / math.sqrt(length))
    kernel = contract("ft,fc->tc", activation, filter_w) * envelope
    tables_all = build_tables(length)
    forward_transform, inverse_transform = staged_forward, staged_inverse
    kernel_spec = forward_transform(kernel, tables_all)
    skip_row = skip[0][None, :]
    weighted_chan, upstream_chan = (
        lax.all_to_all(weighted, "seq", split_axis=1, concat_axis=0, tiled=True),
        lax.all_to_all(upstream, "seq", split_axis=1, concat_axis=0, tiled=True),
    )
    weighted_f = weighted_chan.astype(jnp.float32)
    weighted_spec = forward_transform(weighted_f, tables_all)
    conv = inverse_transform(spectral_product(kernel_spec, weighted_spec, False), tables_all)
    mixed_chan, weighted_f, weighted_spec = (
        (conv + skip_row * weighted_f).astype(jnp.bfloat16),
        weighted_f,
        weighted_spec,
    )
    upstream_f = upstream_chan.astype(jnp.float32)
    upstream_spec = forward_transform(upstream_f, tables_all)
    backward_conv = inverse_transform(
        spectral_product(kernel_spec, upstream_spec, True), tables_all
    )
    grad_chan = (backward_conv + skip_row * upstream_f).astype(jnp.bfloat16)
    grad_skip = jnp.sum(upstream_f * weighted_f, axis=0)
    grad_kernel = inverse_transform(
        spectral_product(weighted_spec, upstream_spec, True), tables_all
    )
    grad_chan, grad_skip, grad_kernel = (grad_chan, grad_skip, grad_kernel)
    mixed_seq, grad_weighted = (
        lax.all_to_all(mixed_chan, "seq", split_axis=0, concat_axis=1, tiled=True),
        lax.all_to_all(grad_chan, "seq", split_axis=0, concat_axis=1, tiled=True),
    )
    output = (gate_second.astype(jnp.float32) * mixed_seq.astype(jnp.float32)).astype(jnp.bfloat16)
    next_input = from_behind(output, "pipe", 1)
    grad_decay = jnp.sum(grad_kernel * kernel * (-positions / length), axis=0)
    grad_raw = grad_kernel * envelope
    grad_filter_w = contract("ft,tc->fc", activation, grad_raw)
    grad_preact = contract("fc,tc->ft", filter_w, grad_raw) * jnp.cos(preact)
    part_weight = contract("et,ft->ef", features, grad_preact)
    part_bias = jnp.sum(grad_preact, axis=1)
    grad_embed_w, grad_embed_b = lax.psum((part_weight, part_bias), "seq")
    grad_values = (grad_weighted.astype(jnp.float32) * gate_first.astype(jnp.float32)).astype(
        jnp.bfloat16
    )
    grad_first = (grad_weighted.astype(jnp.float32) * values.astype(jnp.float32)).astype(
        jnp.bfloat16
    )
    grad_second = (cotangent.astype(jnp.float32) * mixed_seq.astype(jnp.float32)).astype(
        jnp.bfloat16
    )
    moved_values, moved_first, moved_second = from_behind(
        (grad_values, grad_first, grad_second), "pipe", -1
    )
    return (
        next_input[None],
        moved_values[None],
        moved_first[None],
        moved_second[None],
        grad_embed_w[None],
        grad_embed_b[None],
        grad_filter_w[None],
        grad_decay[None],
        grad_skip[None],
    )


def solution(mesh):
    return jax.shard_map(
        per_device,
        mesh=mesh,
        in_specs=(
            P("pipe", "seq", None),
            P("pipe", "seq", None),
            P("pipe", "seq", None),
            P("pipe", "seq", None),
            P("pipe", None, None),
            P("pipe", None),
            P("pipe", None, "seq"),
            P("pipe", "seq"),
            P("pipe", "seq"),
        ),
        out_specs=(
            P("pipe", "seq", None),
            P("pipe", "seq", None),
            P("pipe", "seq", None),
            P("pipe", "seq", None),
            P("pipe", None, None),
            P("pipe", None),
            P("pipe", None, "seq"),
            P("pipe", "seq"),
            P("pipe", "seq"),
        ),
        check_vma=False,
    )
```

```python
import functools
import math

import jax
import jax.numpy as jnp
import numpy as np
from jax import lax
from jax.experimental import pallas as pl
from jax.experimental.pallas import tpu as pltpu
from jax.sharding import PartitionSpec as P

E = 33


def from_behind(value, axis, steps):
    count = lax.axis_size(axis)
    pairs = [(source, (source + steps) % count) for source in range(count)]
    return lax.ppermute(value, axis, pairs)


def contract(form, left, right):
    return jnp.einsum(form, left, right, precision=lax.Precision.HIGHEST)


def position_features(length):
    position_ids = jnp.arange(length, dtype=jnp.int32)
    band_count = (E - 1) // 2
    band_index = jnp.arange(1, band_count + 1, dtype=jnp.int32)
    turn_ids = band_index[:, None] * band_index[:, None] * position_ids[None, :] % length
    angles = 2.0 * math.pi / length * turn_ids.astype(jnp.float32)
    position_ramp = position_ids.astype(jnp.float32)[None, :] / length
    return jnp.concatenate([position_ramp, jnp.cos(angles), jnp.sin(angles)], axis=0)


def build_tables(length):
    fft_total = 2 * length
    outer_len = 128
    half_len = outer_len // 2
    kept_len = half_len + 1
    inner_len = fft_total // outer_len
    index_kept = jnp.arange(kept_len, dtype=jnp.int32)
    index_half = jnp.arange(half_len, dtype=jnp.int32)
    index_inner = jnp.arange(inner_len, dtype=jnp.int32)
    angle_outer = (
        2.0
        * math.pi
        / outer_len
        * (index_kept[:, None] * index_half[None, :] % outer_len).astype(jnp.float32)
    )
    cos_outer = jnp.cos(angle_outer)
    sin_outer = jnp.sin(angle_outer)
    table_first = jnp.concatenate([cos_outer, -sin_outer], axis=0)
    angle_twist = (
        2.0
        * math.pi
        / fft_total
        * (index_kept[:, None] * index_inner[None, :] % fft_total).astype(jnp.float32)
    )
    cos_twist = jnp.cos(angle_twist)[:, :, None]
    sin_twist = jnp.sin(angle_twist)[:, :, None]
    angle_inner = (
        2.0
        * math.pi
        / inner_len
        * (index_inner[:, None] * index_inner[None, :] % inner_len).astype(jnp.float32)
    )
    cos_inner = jnp.cos(angle_inner)
    sin_inner = jnp.sin(angle_inner)
    table_second = jnp.stack(
        [jnp.stack([cos_inner, sin_inner], axis=1), jnp.stack([-sin_inner, cos_inner], axis=1)],
        axis=0,
    )
    table_back = jnp.stack(
        [jnp.stack([cos_inner, -sin_inner], axis=1), jnp.stack([sin_inner, cos_inner], axis=1)],
        axis=0,
    )
    weight_kept = (
        jnp.where((index_kept == 0) | (index_kept == half_len), 1.0, 2.0).astype(jnp.float32)
        / fft_total
    )
    table_last = jnp.stack(
        [
            jnp.transpose(cos_outer) * weight_kept[None, :],
            -jnp.transpose(sin_outer) * weight_kept[None, :],
        ],
        axis=1,
    )
    return (
        table_first,
        cos_twist,
        sin_twist,
        table_second,
        table_back,
        table_last,
        half_len,
        kept_len,
        inner_len,
    )


def staged_forward(field, tables_all):
    (
        table_first,
        cos_twist,
        sin_twist,
        table_second,
        table_back,
        table_last,
        half_len,
        kept_len,
        inner_len,
    ) = tables_all
    columns = field.shape[1]
    shaped = field.reshape(half_len, inner_len, columns)
    stacked = contract("kn,npc->kpc", table_first, shaped)
    part_re = stacked[:kept_len]
    part_im = stacked[kept_len:]
    twisted = jnp.stack(
        [part_re * cos_twist + part_im * sin_twist, part_im * cos_twist - part_re * sin_twist],
        axis=0,
    )
    return contract("sqrp,rkpc->skqc", table_second, twisted)


def staged_inverse(spec, tables_all):
    (
        table_first,
        cos_twist,
        sin_twist,
        table_second,
        table_back,
        table_last,
        half_len,
        kept_len,
        inner_len,
    ) = tables_all
    columns = spec.shape[3]
    sectioned = contract("sprq,rkqc->skpc", table_back, spec)
    section_re = sectioned[0]
    section_im = sectioned[1]
    twisted = jnp.stack(
        [
            section_re * cos_twist - section_im * sin_twist,
            section_im * cos_twist + section_re * sin_twist,
        ],
        axis=0,
    )
    result = contract("nrk,rkpc->npc", table_last, twisted)
    return result.reshape(half_len * inner_len, columns)


ROWS = 128
LEVEL = 2 * ROWS
PADDED = 40
LEVELS = 4
CW = 256
AHEAD = 5
TILE = 16


def level_tables():
    odd = 2 * np.arange(LEVEL) + 1
    shift = np.arange(-LEVEL, LEVEL)
    unit = math.pi / (2 * LEVEL)
    angle = unit * ((odd[:, None] * shift[None]) % (4 * LEVEL))
    ahead = np.concatenate([np.cos(angle), -np.sin(angle)], axis=0)
    back = ahead.T / LEVEL
    back = np.concatenate([back[LEVEL:], back[:LEVEL]], axis=1)
    return jnp.asarray(ahead, jnp.bfloat16), jnp.asarray(back, jnp.bfloat16)


def padded_features(length):
    position = np.arange(length)
    band = np.arange(1, (E - 1) // 2 + 1)
    angle = 2.0 * math.pi / length * ((band[:, None] ** 2 * position[None]) % length)
    table = np.zeros((PADDED, length), np.float32)
    table[0] = position / length
    table[1 : 1 + len(band)] = np.cos(angle)
    table[1 + len(band) : E] = np.sin(angle)
    table[E] = 1.0
    return table


def section_kernel(
    pipes, per,
    v_in, g1_in, og_in, g2_in, feat_in, feat_t_in, ahead_in, back_in,
    wf, decay, skip, w_embed, bias,
    o_next, o_val, o_first, o_second, o_emb, o_wf, o_decay, o_skip,
    ins, feat, feat_t, ahead, back, ahead_k, back_g, wext, act, act_t, cos_t,
    wf_all, row_all, lev, ysend, near1, far1, far2, cin, cout, olev, landed,
    stage, fpart, kb, env, kap, spec, prod, corr, graw, gact,
    keep, sums_out, relayed, sums_in, part, parts,
    loaded, y_s, y_r, z_s, z_r, c_s, c_r, h_s, h_r, p_s, p_r,
    wf_s, wf_r, row_s, row_r, k_s, k_r, q_r, x_s, x_r,
):
    f32, bf16 = jnp.float32, jnp.bfloat16
    length = LEVELS * LEVEL
    width = wf.shape[1]
    hidden = wf.shape[0]
    shards = 2 * LEVELS
    steps = LEVELS * per
    pipe = lax.axis_index("pipe")
    me = lax.axis_index("seq")
    z, y = me // 2, me % 2
    twin = 1 - y
    partner = 2 * z + twin
    near = z // 2
    far = 1 - near
    adjacent = z + 1 - 2 * (z % 2)
    inner = (z == 1) | (z == 2)
    outer = (z == 0) | (z == 3)
    nxt = (pipe + 1) % pipes
    prv = (pipe + pipes - 1) % pipes
    high = lax.Precision.HIGHEST
    sign = (1 - 2 * near).astype(f32)

    def rows(index):
        return pl.ds(pl.multiple_of(index * ROWS, ROWS), ROWS)

    def cols(step, lane):
        block = (2 * (step // per) + lane) * per + step % per
        return pl.ds(pl.multiple_of(block * CW, CW), CW)

    def sub(step):
        return pl.ds(pl.multiple_of((step % per) * CW, CW), CW)

    def remote(src, dst, send, recv, there):
        return pltpu.make_async_remote_copy(
            src_ref=src, dst_ref=dst, send_sem=send, recv_sem=recv, device_id=there,
            device_id_type=pl.DeviceIdType.MESH,
        )

    def at_level(level):
        return (pipe, 2 * level + y)

    def crossing(kind, step):
        return remote(
            ysend.at[kind, step], lev.at[kind, step, rows(y), :],
            y_s, y_r.at[kind, step], (pipe, partner),
        )

    def crossed(kind, step):
        return remote(
            ysend.at[kind, step], lev.at[kind, step, rows(twin), :],
            y_s, y_r.at[kind, step], (pipe, partner),
        )

    def upward(slot, step, buffer, level, send):
        return remote(
            lev.at[near, step], buffer.at[step], z_s.at[send], z_r.at[slot, step],
            at_level(level),
        )

    def given(step):
        return remote(
            cout.at[step], cin.at[step], c_s, c_r.at[step], at_level(adjacent)
        )

    def homeward(kind, step):
        return remote(
            olev.at[kind, step, rows(twin), :], landed.at[kind, step], h_s, h_r.at[kind, step],
            (pipe, partner),
        )

    def handed(kind, side, step):
        out = (o_next, o_second, o_val, o_first)[kind]
        lane = (y, twin)[side]
        return remote(
            stage.at[kind, side, step], out.at[:, cols(step, lane)],
            p_s.at[kind], p_r.at[kind], (prv if kind else nxt, me),
        )

    def filters(there, source):
        return (
            remote(wf_all.at[source], wf_all.at[source], wf_s, wf_r.at[source],
                   at_level(there)),
            remote(row_all.at[source], row_all.at[source], row_s, row_r.at[source],
                   at_level(there)),
        )

    def relay(step):
        return remote(
            sums_out.at[step], relayed.at[step], k_s, q_r.at[step], at_level(adjacent)
        )

    def owed(step, slot, level):
        return remote(
            sums_out.at[step], sums_in.at[slot, step % per], k_s,
            k_r.at[slot, step % per], at_level(level),
        )

    def shared(there, source):
        return remote(part, parts.at[source], x_s, x_r, (pipe, there))

    def other_levels(visit):
        def body(step, carry):
            visit((z + 1 + step) % LEVELS)
            return carry

        lax.fori_loop(0, LEVELS - 1, body, 0)

    def others(visit):
        def body(step, carry):
            visit((me + 1 + step) % shards)
            return carry

        lax.fori_loop(0, shards - 1, body, 0)

    def every(visit):
        def body(step, carry):
            visit(step)
            return carry

        lax.fori_loop(0, steps, body, 0)

    loads = [
        pltpu.make_async_copy(src, dst, loaded.at[index])
        for index, (src, dst) in enumerate((
            (v_in, ins.at[0]), (g1_in, ins.at[1]), (og_in, ins.at[2]), (g2_in, ins.at[3]),
            (feat_in, feat), (feat_t_in, feat_t), (ahead_in, ahead), (back_in, back),
        ))
    ]
    for load in loads[:4]:
        load.start()
    barrier = pltpu.get_barrier_semaphore()

    def greet(there):
        pl.semaphore_signal(
            barrier, inc=1, device_id=(pipe, there), device_id_type=pl.DeviceIdType.MESH
        )

    others(greet)
    for beside in (nxt, prv):
        pl.semaphore_signal(
            barrier, inc=1, device_id=(beside, me), device_id_type=pl.DeviceIdType.MESH
        )
    wf_all[z] = wf[...].astype(bf16)
    row_all[z, 0:1, :] = decay[...]
    row_all[z, 1:2, :] = skip[...]
    def times(kind, here):
        left, right = ins[2 * kind, :, here], ins[2 * kind + 1, :, here]
        return (left.astype(f32) * right.astype(f32)).astype(bf16)

    def weigh(step):
        for kind in (0, 1):
            ysend[kind, step] = times(kind, cols(step, twin))
            lev[kind, step, rows(y), :] = times(kind, cols(step, y))

    pl.semaphore_wait(barrier, shards + 1)

    def send_filters(there):
        for copy in filters(there, z):
            copy.start()

    def cross(step):
        crossing(near, step).start()
        crossing(far, step).start()

    other_levels(send_filters)
    for load in loads[:4]:
        load.wait()
    weigh(0)
    cross(0)

    def weigh_and_cross(step, carry):
        weigh(step)
        cross(step)
        return carry

    for load in loads[4:]:
        load.start()
    lax.fori_loop(1, steps, weigh_and_cross, 0)
    wext[...] = jnp.zeros_like(wext)
    wext[:E, :hidden] = w_embed[:, 0, :]
    wext[:E, hidden:] = w_embed[:, 0, :]
    wext[E : E + 1, :hidden] = bias[...]
    wext[E : E + 1, hidden:] = bias[...]
    kb[:LEVEL, :] = jnp.zeros((LEVEL, CW), bf16)
    gact[...] = jnp.zeros_like(gact)

    def climb(step):
        crossed(near, step).wait_recv()

        @pl.when(inner)
        def _():
            upward(1, step, far1, 3 - z, 0).start()

        @pl.when(outer)
        def _():
            upward(2, step, far2, 3 - adjacent, 1).start()
            upward(0, step, near1, adjacent, 0).start()

    climb(0)
    for load in loads[4:]:
        load.wait()
    ahead_k[:LEVEL, :] = ahead[:LEVEL, :]
    ahead_k[LEVEL:, :] = (ahead[LEVEL:, :].astype(f32) * sign).astype(bf16)
    for block in range(4):
        here = slice(block * LEVEL, (block + 1) * LEVEL)
        flip = sign if block % 2 else 1.0
        back_g[:, here] = (back[:, here].astype(f32) * flip).astype(bf16)

    def activate(block, carry):
        here = pl.ds(pl.multiple_of(block * LEVEL, LEVEL), LEVEL)
        lane = lax.broadcasted_iota(jnp.int32, (LEVEL, 2 * hidden), 1)
        value = jnp.sin(jnp.dot(feat_t[here, :], wext[...], precision=high))
        top = value.astype(bf16).astype(f32)
        act[here, :] = jnp.where(lane < hidden, top, value - top).astype(bf16)
        line = lax.broadcasted_iota(jnp.int32, (2 * hidden, LEVEL), 0)
        preact = lax.dot_general(
            wext[...], feat[:, here], (((0,), (0,)), ((), ())), precision=high
        )
        value = jnp.sin(preact)
        top = value.astype(bf16).astype(f32)
        act_t[:, here] = jnp.where(line < hidden, top, value - top).astype(bf16)
        cos_t[:, here] = jnp.cos(preact[:hidden])
        return carry

    lax.fori_loop(0, LEVELS, activate, 0)
    for step in range(1, AHEAD):
        climb(step)

    def land_filters(there):
        for copy in filters(there, there):
            copy.wait_recv()

    other_levels(land_filters)

    def filter_rows(step):
        return wf_all[step // per, :, sub(step)]

    def prepare(step, depth):
        weights = filter_rows(step)
        weights = jnp.concatenate([weights, weights], axis=0)
        rate = row_all[step // per, 0:1, sub(step)]
        fine = lax.broadcasted_iota(jnp.int32, (LEVEL, 1), 0).astype(f32)
        base = jnp.exp(-rate * fine / length) * (1.0 / math.sqrt(length))
        for block in range(depth):
            here = slice(block * LEVEL, (block + 1) * LEVEL)
            raw = jnp.dot(act[here, :], weights, preferred_element_type=f32)
            envelope = base * jnp.exp(rate * (-block * LEVEL / length)) if block else base
            env[here, :] = envelope
            kb[(block + 1) * LEVEL : (block + 2) * LEVEL, :] = (raw * envelope).astype(bf16)
        kap[0] = jnp.dot(
            ahead_k[:, LEVEL:], kb[LEVEL : 2 * LEVEL, :], preferred_element_type=f32
        )
        for block in range(1, depth):
            kap[block] = jnp.dot(
                ahead_k[...], kb[block * LEVEL : (block + 2) * LEVEL, :],
                preferred_element_type=f32,
            )

    def transform(slot, source):
        spec[slot] = jnp.dot(ahead[:, LEVEL:], source, preferred_element_type=f32)

    def inverse(slot):
        return jnp.dot(back[:, : 2 * LEVEL], prod[slot], preferred_element_type=f32)

    def forth(one, two):
        return one[0] * two[0] - one[1] * two[1], one[0] * two[1] + one[1] * two[0]

    def conj(one, two):
        return one[0] * two[0] + one[1] * two[1], one[0] * two[1] - one[1] * two[0]

    def add(*terms):
        total = terms[0]
        for term in terms[1:]:
            total = total[0] + term[0], total[1] + term[1]
        return total

    def half(one):
        return one[0] * 0.5, one[1] * 0.5

    def combine(visit):
        def body(tile, carry):
            top = pl.ds(pl.multiple_of(tile * TILE, TILE), TILE)
            low = pl.ds(pl.multiple_of(LEVEL + tile * TILE, TILE), TILE)

            def read(ref, index):
                return ref[index, top, :], ref[index, low, :]

            def write(ref, index, value):
                ref[index, top, :] = value[0].astype(bf16)
                ref[index, low, :] = value[1].astype(bf16)

            visit(read, write)
            return carry

        lax.fori_loop(0, LEVEL // TILE, body, 0, unroll=4)

    def combine_given(read, write):
        k1, k2, k3 = [read(kap, index) for index in range(1, 4)]
        f0, f1, f2 = [read(spec, index) for index in range(2, 5)]
        write(prod, 0, add(conj(k1, f0), conj(k2, f1), conj(k3, f2)))

    def combine_inner(read, write):
        k0, k1, k2 = [read(kap, index) for index in range(3)]
        n0, n1, f0, f1, f2 = [read(spec, index) for index in range(5)]
        write(prod, 1, add(forth(k0, n0), forth(k1, n1)))
        write(prod, 2, add(conj(k0, f0), conj(k1, f1), conj(k2, f2)))
        write(corr, 0, conj(n0, f0))
        write(corr, 1, add(conj(n1, f0), conj(n0, half(f1))))
        write(corr, 2, conj(n0, f2))
        write(corr, 3, conj(half(n1), f2))

    def combine_outer(read, write):
        k0, n0, f0 = read(kap, 0), read(spec, 0), read(spec, 2)
        write(prod, 1, forth(k0, n0))
        write(prod, 2, conj(k0, f0))
        write(corr, 0, conj(n0, f0))

    def skipped(kind, step):
        return row_all[step // per, 1:2, sub(step)] * lev[kind, step].astype(f32)

    def pass_on(kind, side, step):
        lane = (y, twin)[side]
        block = (olev[kind, step, rows(y), :] if side == 0 else landed[kind, step]).astype(f32)
        here = cols(step, lane)
        for way, source in ((0, 3), (1, 2)) if kind == 0 else ((2, 1), (3, 0)):
            stage[way, side, step] = (ins[source, :, here].astype(f32) * block).astype(bf16)
            handed(way, side, step).start()

    def send_out(kind, step):
        homeward(kind, step).start()
        pass_on(kind, 0, step)

    def land(step):
        for kind in (0, 1):
            homeward(kind, step).wait_recv()
            pass_on(kind, 1, step)

    def correlate(step, depth):
        fine = lax.broadcasted_iota(jnp.int32, (LEVEL, 1), 0).astype(f32)
        total = jnp.zeros((1, CW), f32)
        for block in range(depth):
            here = slice(block * LEVEL, (block + 1) * LEVEL)
            grad = jnp.dot(back_g[:, : 2 * LEVEL], corr[block], preferred_element_type=f32)
            if block + 1 < depth:
                grad += jnp.dot(
                    back_g[:, 2 * LEVEL :], corr[block + 1], preferred_element_type=f32
                )
            graw[here, :] = (grad * env[here, :]).astype(bf16)
            kernel = kb[(block + 1) * LEVEL : (block + 2) * LEVEL, :].astype(f32)
            place = (fine + block * LEVEL) * (-1.0 / length)
            total += jnp.sum(grad * kernel * place, axis=0, keepdims=True)
        both = lev[0, step].astype(f32) * lev[1, step].astype(f32)
        skip_sum = jnp.sum(both, axis=0, keepdims=True)
        span = depth * LEVEL
        both = jnp.dot(act_t[:, :span], graw[:span, :], preferred_element_type=f32)
        share = both[:hidden] + both[hidden:]
        gact[:, :span] += lax.dot_general(
            filter_rows(step), graw[:span, :], (((1,), (1,)), ((), ())),
            preferred_element_type=f32,
        )
        keep[step, :hidden, :] = share
        keep[step, hidden : hidden + 2, :] = jnp.concatenate([total, skip_sum], axis=0)
        owner = step // per

        @pl.when(owner == adjacent)
        def _():
            pack(step, keep[step])
            owed(step, 0, adjacent).start()

        @pl.when(outer & (owner // 2 != near))
        def _():
            pack(step, keep[step])
            relay(step).start()

    def pack(step, value):
        pair = value[hidden : hidden + 2]
        top = pair.astype(bf16).astype(f32)
        tail = jnp.concatenate([top, pair - top, jnp.zeros((12, CW), f32)], axis=0)
        sums_out[step] = jnp.concatenate([value[:hidden], tail], axis=0).astype(bf16)

    def unpack(ref, *index):
        value = ref[index].astype(f32)
        tail = value[hidden:]
        return value[:hidden], tail[0:2] + tail[2:4]

    def pay(step):
        @pl.when((step // per) // 2 != near)
        def _():
            relay(step).wait_recv()
            value, pair = unpack(relayed, step)
            keep[step, :hidden, :] += value
            keep[step, hidden : hidden + 2, :] += pair
            pack(step, keep[step])
            owed(step, 1, step // per).start()

    def climb_later(step):
        @pl.when(step + AHEAD < steps)
        def _():
            climb(step + AHEAD)

    def reduce_embed():
        grad_pre = gact[...] * cos_t[...]
        part[...] = lax.dot_general(
            feat[...], jnp.concatenate([grad_pre, jnp.zeros_like(grad_pre)], axis=0),
            (((1,), (1,)), ((), ())), precision=high,
        )
        others(lambda there: shared(there, me).start())
        parts[me] = part[...]

    @pl.when(inner)
    def _():
        def turn(step):
            climb_later(step)
            prepare(step, LEVELS)
            transform(0, lev[near, step])
            crossed(far, step).wait_recv()
            transform(2, lev[far, step])
            upward(0, step, near1, adjacent, 0).wait_recv()
            transform(1, near1[step])
            upward(1, step, far1, 3 - z, 0).wait_recv()
            transform(3, far1[step])
            upward(2, step, far2, 3 - adjacent, 0).wait_recv()
            transform(4, far2[step])
            combine(combine_given)
            cout[step] = inverse(0).astype(bf16)
            given(step).start()
            combine(combine_inner)
            olev[near, step] = (inverse(1) + skipped(near, step)).astype(bf16)
            olev[far, step] = (inverse(2) + skipped(far, step)).astype(bf16)
            send_out(0, step)
            send_out(1, step)

            correlate(step, LEVELS)

            @pl.when(step >= 1)
            def _():
                land(step - 1)

        every(turn)
        every(pay)
        reduce_embed()
        land(steps - 1)

    @pl.when(outer)
    def _():
        def settle(step):
            given(step).wait_recv()
            olev[far, step] = (fpart[step % 2] + cin[step].astype(f32)).astype(bf16)

            @pl.when(near == 0)
            def _():
                send_out(1, step)

            @pl.when(near == 1)
            def _():
                send_out(0, step)

        def turn(step):
            climb_later(step)
            prepare(step, 1)
            transform(0, lev[near, step])
            crossed(far, step).wait_recv()
            transform(2, lev[far, step])
            combine(combine_outer)
            olev[near, step] = (inverse(1) + skipped(near, step)).astype(bf16)

            @pl.when(near == 0)
            def _():
                send_out(0, step)

            @pl.when(near == 1)
            def _():
                send_out(1, step)

            fpart[step % 2] = inverse(2) + skipped(far, step)
            correlate(step, 1)

            @pl.when(step >= 1)
            def _():
                settle(step - 1)

            @pl.when(step >= 2)
            def _():
                land(step - 2)

        every(turn)
        reduce_embed()
        settle(steps - 1)
        land(steps - 2)
        land(steps - 1)

    for piece in range(per):
        here = slice(piece * CW, (piece + 1) * CW)
        step = z * per + piece
        value, pair = keep[step, :hidden, :], keep[step, hidden : hidden + 2, :]
        for slot in range(2):
            owed(step, slot, z).wait_recv()
            more, more_pair = unpack(sums_in, slot, piece)
            value, pair = value + more, pair + more_pair
        o_wf[:, here] = value
        o_decay[:, here] = pair[0:1]
        o_skip[:, here] = pair[1:2]

    remote(part, parts.at[: shards - 1], x_s, x_r, (pipe, partner)).wait_recv()
    total = parts[0]
    for index in range(1, shards):
        total = total + parts[index]
    o_emb[...] = total

    def all_sent(source, sem):
        remote(source, source, sem, sem, (pipe, partner)).wait_send()

    all_sent(wf_all.at[: LEVELS - 1], wf_s)
    all_sent(row_all.at[: LEVELS - 1], row_s)
    all_sent(ysend, y_s)
    all_sent(landed, h_s)
    all_sent(sums_out.at[: steps - per], k_s)
    all_sent(parts.at[: shards - 1], x_s)
    for kind, out in enumerate((o_next, o_second, o_val, o_first)):
        all_sent(stage.at[kind], p_s.at[kind])
        remote(out, out, p_s.at[kind], p_r.at[kind], (pipe, partner)).wait_recv()
    all_sent(far1, z_s.at[0])

    @pl.when(inner)
    def _():
        all_sent(cout, c_s)

    @pl.when(outer)
    def _():
        all_sent(far1, z_s.at[1])


VMEM_MAIN = 58 * 1024 * 1024
VMEM_FINISH = 8 * 1024 * 1024


def finish_kernel(
    a_in, b_in, c_in, d_in, emb, wf, row_d, row_s,
    a_out, b_out, c_out, d_out, o_emb, o_bias, o_wf, o_d, o_s, put,
):
    writes = [
        pltpu.make_async_copy(src, dst.at[0], put.at[kind])
        for kind, (src, dst) in enumerate(
            ((a_in, a_out), (b_in, b_out), (c_in, c_out), (d_in, d_out))
        )
    ]
    for write in writes:
        write.start()
    o_emb[:, 0, :] = emb[:E, : o_emb.shape[2]]
    o_bias[...] = emb[E : E + 1, : o_bias.shape[1]]
    o_wf[0] = wf[...]
    o_d[...] = row_d[...]
    o_s[...] = row_s[...]
    for write in writes:
        write.wait()


def fused_section(v, g1, g2, og, w_embed, b_embed, wf, decay, skip):
    pipes = lax.axis_size("pipe")
    shards = 2 * LEVELS
    length = LEVELS * LEVEL
    wide_cols = v.shape[1]
    hidden, width = wf.shape
    per = width // CW
    steps = LEVELS * per
    f32, bf16 = jnp.float32, jnp.bfloat16
    feat = padded_features(length)
    ahead, back = level_tables()
    vmem = pl.BlockSpec(memory_space=pltpu.VMEM)
    hbm = pl.BlockSpec(memory_space=pl.ANY)
    stream = pltpu.VMEM((ROWS, wide_cols), bf16)
    row = jax.ShapeDtypeStruct((1, width), f32)
    dma = pltpu.SemaphoreType.DMA
    level = pltpu.VMEM((steps, LEVEL, CW), bf16)
    results = pl.pallas_call(
        functools.partial(section_kernel, pipes, per),
        out_shape=(
            stream, stream, stream, stream,
            pltpu.VMEM((PADDED, 2 * hidden), f32),
            pltpu.VMEM((hidden, width), f32), pltpu.VMEM((1, width), f32),
            pltpu.VMEM((1, width), f32),
        ),
        in_specs=[hbm] * 8 + [vmem] * 5,
        out_specs=(vmem,) * 8,
        scratch_shapes=[
            pltpu.VMEM((4, ROWS, wide_cols), bf16),
            pltpu.VMEM((PADDED, length), f32),
            pltpu.VMEM((length, PADDED), f32),
            pltpu.VMEM((2 * LEVEL, 2 * LEVEL), bf16),
            pltpu.VMEM((LEVEL, 4 * LEVEL), bf16),
            pltpu.VMEM((2 * LEVEL, 2 * LEVEL), bf16),
            pltpu.VMEM((LEVEL, 4 * LEVEL), bf16),
            pltpu.VMEM((PADDED, 2 * hidden), f32),
            pltpu.VMEM((length, 2 * hidden), bf16),
            pltpu.VMEM((2 * hidden, length), bf16),
            pltpu.VMEM((hidden, length), f32),
            pltpu.VMEM((LEVELS, hidden, width), bf16),
            pltpu.VMEM((LEVELS, 8, width), f32),
            pltpu.VMEM((2, steps, LEVEL, CW), bf16),
            pltpu.VMEM((2, steps, ROWS, CW), bf16),
            level, level, level, level, level,
            pltpu.VMEM((2, steps, LEVEL, CW), bf16),
            pltpu.VMEM((2, steps, ROWS, CW), bf16),
            pltpu.VMEM((4, 2, steps, ROWS, CW), bf16),
            pltpu.VMEM((2, LEVEL, CW), f32),
            pltpu.VMEM((length + LEVEL, CW), bf16),
            pltpu.VMEM((length, CW), f32),
            pltpu.VMEM((LEVELS, 2 * LEVEL, CW), f32),
            pltpu.VMEM((5, 2 * LEVEL, CW), f32),
            pltpu.VMEM((3, 2 * LEVEL, CW), bf16),
            pltpu.VMEM((LEVELS, 2 * LEVEL, CW), bf16),
            pltpu.VMEM((length, CW), bf16),
            pltpu.VMEM((hidden, length), f32),
            pltpu.VMEM((steps, hidden + 8, CW), f32),
            pltpu.VMEM((steps, hidden + 16, CW), bf16),
            pltpu.VMEM((steps, hidden + 16, CW), bf16),
            pltpu.VMEM((2, per, hidden + 16, CW), bf16),
            pltpu.VMEM((PADDED, 2 * hidden), f32),
            pltpu.VMEM((shards, PADDED, 2 * hidden), f32),
            dma((8,)),
            dma, dma((2, steps)),
            dma((2,)), dma((3, steps)),
            dma, dma((steps,)),
            dma, dma((2, steps)),
            dma((4,)), dma((4,)),
            dma, dma((LEVELS,)),
            dma, dma((LEVELS,)),
            dma, dma((2, per)), dma((steps,)),
            dma, dma,
        ],
        compiler_params=pltpu.CompilerParams(
            collective_id=0, has_side_effects=True, vmem_limit_bytes=VMEM_MAIN
        ),
    )(
        v, g1, og, g2, jnp.asarray(feat), jnp.asarray(feat.T.copy()), ahead, back,
        wf, decay[None], skip[None], w_embed[:, None, :], b_embed[None],
    )
    results = [pltpu.with_memory_space_constraint(result, pltpu.VMEM) for result in results]
    final = jax.ShapeDtypeStruct((1, ROWS, wide_cols), bf16)
    done = pl.pallas_call(
        finish_kernel,
        out_shape=(
            final, final, final, final,
            jax.ShapeDtypeStruct((E, 1, hidden), f32),
            jax.ShapeDtypeStruct((1, hidden), f32),
            jax.ShapeDtypeStruct((1, hidden, width), f32), row, row,
        ),
        in_specs=[hbm] * 4 + [vmem] * 4,
        out_specs=(hbm,) * 4 + (vmem,) * 5,
        scratch_shapes=[dma((4,))],
        compiler_params=pltpu.CompilerParams(vmem_limit_bytes=VMEM_FINISH),
    )(*results)
    return done[:4] + (jnp.swapaxes(done[4], 0, 1),) + done[5:]


def spectral_product(left, right, conjugate_left):
    left_re = left[0]
    left_im = left[1]
    right_re = right[0]
    right_im = right[1]
    if conjugate_left:
        left_im = -left_im
    return jnp.stack(
        [left_re * right_re - left_im * right_im, left_re * right_im + left_im * right_re], axis=0
    )


def per_device(value_in, gate_one, gate_two, out_grad, w_embed, b_embed, w_filter, decay, skip):
    values = value_in[0]
    gate_first = gate_one[0]
    gate_second = gate_two[0]
    cotangent = out_grad[0]
    filter_w = w_filter[0]
    shards = lax.axis_size("seq")
    length = values.shape[0] * shards
    fits = length == 1024 and values.shape == (ROWS, 4096) and shards == 8
    if fits and lax.axis_size("pipe") > 2:
        return fused_section(
            values, gate_first, gate_second, cotangent,
            w_embed[0], b_embed[0], filter_w, decay[0], skip[0],
        )
    weighted = (values.astype(jnp.float32) * gate_first.astype(jnp.float32)).astype(jnp.bfloat16)
    upstream = (cotangent.astype(jnp.float32) * gate_second.astype(jnp.float32)).astype(
        jnp.bfloat16
    )
    features = position_features(length)
    preact = contract("ef,et->ft", w_embed[0], features) + b_embed[0][:, None]
    activation = jnp.sin(preact)
    positions = jnp.arange(length, dtype=jnp.int32).astype(jnp.float32)[:, None]
    envelope = jnp.exp(-decay[0][None, :] * positions / length) * (1.0 / math.sqrt(length))
    kernel = contract("ft,fc->tc", activation, filter_w) * envelope
    tables_all = build_tables(length)
    forward_transform, inverse_transform = staged_forward, staged_inverse
    kernel_spec = forward_transform(kernel, tables_all)
    skip_row = skip[0][None, :]
    weighted_chan, upstream_chan = (
        lax.all_to_all(weighted, "seq", split_axis=1, concat_axis=0, tiled=True),
        lax.all_to_all(upstream, "seq", split_axis=1, concat_axis=0, tiled=True),
    )
    weighted_f = weighted_chan.astype(jnp.float32)
    weighted_spec = forward_transform(weighted_f, tables_all)
    conv = inverse_transform(spectral_product(kernel_spec, weighted_spec, False), tables_all)
    mixed_chan, weighted_f, weighted_spec = (
        (conv + skip_row * weighted_f).astype(jnp.bfloat16),
        weighted_f,
        weighted_spec,
    )
    upstream_f = upstream_chan.astype(jnp.float32)
    upstream_spec = forward_transform(upstream_f, tables_all)
    backward_conv = inverse_transform(
        spectral_product(kernel_spec, upstream_spec, True), tables_all
    )
    grad_chan = (backward_conv + skip_row * upstream_f).astype(jnp.bfloat16)
    grad_skip = jnp.sum(upstream_f * weighted_f, axis=0)
    grad_kernel = inverse_transform(
        spectral_product(weighted_spec, upstream_spec, True), tables_all
    )
    grad_chan, grad_skip, grad_kernel = (grad_chan, grad_skip, grad_kernel)
    mixed_seq, grad_weighted = (
        lax.all_to_all(mixed_chan, "seq", split_axis=0, concat_axis=1, tiled=True),
        lax.all_to_all(grad_chan, "seq", split_axis=0, concat_axis=1, tiled=True),
    )
    output = (gate_second.astype(jnp.float32) * mixed_seq.astype(jnp.float32)).astype(jnp.bfloat16)
    next_input = from_behind(output, "pipe", 1)
    grad_decay = jnp.sum(grad_kernel * kernel * (-positions / length), axis=0)
    grad_raw = grad_kernel * envelope
    grad_filter_w = contract("ft,tc->fc", activation, grad_raw)
    grad_preact = contract("fc,tc->ft", filter_w, grad_raw) * jnp.cos(preact)
    part_weight = contract("et,ft->ef", features, grad_preact)
    part_bias = jnp.sum(grad_preact, axis=1)
    grad_embed_w, grad_embed_b = lax.psum((part_weight, part_bias), "seq")
    grad_values = (grad_weighted.astype(jnp.float32) * gate_first.astype(jnp.float32)).astype(
        jnp.bfloat16
    )
    grad_first = (grad_weighted.astype(jnp.float32) * values.astype(jnp.float32)).astype(
        jnp.bfloat16
    )
    grad_second = (cotangent.astype(jnp.float32) * mixed_seq.astype(jnp.float32)).astype(
        jnp.bfloat16
    )
    moved_values, moved_first, moved_second = from_behind(
        (grad_values, grad_first, grad_second), "pipe", -1
    )
    return (
        next_input[None],
        moved_values[None],
        moved_first[None],
        moved_second[None],
        grad_embed_w[None],
        grad_embed_b[None],
        grad_filter_w[None],
        grad_decay[None],
        grad_skip[None],
    )


def solution(mesh):
    return jax.shard_map(
        per_device,
        mesh=mesh,
        in_specs=(
            P("pipe", "seq", None),
            P("pipe", "seq", None),
            P("pipe", "seq", None),
            P("pipe", "seq", None),
            P("pipe", None, None),
            P("pipe", None),
            P("pipe", None, "seq"),
            P("pipe", "seq"),
            P("pipe", "seq"),
        ),
        out_specs=(
            P("pipe", "seq", None),
            P("pipe", "seq", None),
            P("pipe", "seq", None),
            P("pipe", "seq", None),
            P("pipe", None, None),
            P("pipe", None),
            P("pipe", None, "seq"),
            P("pipe", "seq"),
            P("pipe", "seq"),
        ),
        check_vma=False,
    )
```
